32 devices in a mesh: group: 1, expert: 32 (over z, y, x, core).
Axes of the slice: x: 2, y: 2, z: 4, core: 2. Of those that a mesh axis runs over, the one named last changes fastest.
Arguments:
- hidden_state: bfloat16 [256, 2048], P(('group', 'expert')), may hold values from -6 to 6
- cross_query: bfloat16 [256, 2048], P(('group', 'expert')), may hold values from -62 to 62
- source_keys: bfloat16 [256, 64, 2048], P(('group', 'expert')), may hold values from -3 to 3
- source_values: bfloat16 [256, 64, 2048], P(('group', 'expert')), may hold values from -6 to 6
- src_lengths: int32 [256], P(('group', 'expert')), may hold values from 2 to 64
- norm_gain: float32 [2048], replicated, may hold values from 0.5 to 1.5
- w_in: bfloat16 [2048, 16384], P(None, 'expert'), may hold values from -0.125 to 0.125
- w_out: bfloat16 [16384, 2048], P('expert'), may hold values from -0.09375 to 0.09375
- expert_ids: int32 [256, 2], P(('group', 'expert')), may hold values from 0 to 3, all different within a row; in each aligned block of 8 rows (0 to 7, 8 to 15, ...) at most 8 rows name the same one
- route_weights: float32 [256, 2], P(('group', 'expert')), may hold values from 0.2 to 1
Outputs:
- layer_out: bfloat16 [256, 2048], P(('group', 'expert'))
The draws below stay inside these ranges and needn't reach their ends.
Inputs may be any that keep to these rules, and one draw needn't show every extreme that they name: `expert_ids`: each row names two different experts. Among the rows of one device (aligned blocks of 8 streams) no expert is named by more than 8 rows, and in every draw some expert is named by exactly 8 rows of some device.
All inputs are finite; a program needn't handle non-finite values.
Results may differ from the reference program's by a relative error of at most 0.0042.
Values may be sent and summed in bfloat16 or wider, within the bound.
No kernel may reach another device: no remote copies, remote signals or barrier semaphores. Data moves between devices by JAX's collectives and lax.ppermute only.
A program may use at most 64 MiB of HBM per device.

```python
import math
import jax
import jax.numpy as jnp
import numpy as np
from jax import lax

D = 2048
HEADS = 16
FF = 4096
STREAMS_DEV = 8
SRC = 64
EXPERTS = 4
CAP = 8
STREAMS = 256
N_EXPERT = 32


def joint_draw(key):
    query_key = jax.random.fold_in(key, 11)
    cache_key = jax.random.fold_in(key, 12)
    queries = jax.random.truncated_normal(query_key, -3.0, 3.0, (STREAMS, D), jnp.float32)
    keys = jax.random.truncated_normal(cache_key, -3.0, 3.0, (STREAMS, SRC, D), jnp.float32)
    return (queries, keys)


def draw_cross_query(key, part):
    return joint_draw(key)[0].astype(jnp.bfloat16)


def draw_source_keys(key, part):
    return joint_draw(key)[1].astype(jnp.bfloat16)


def place_ends(entries, stream_key, low, high):
    shape = entries.shape
    place = [jax.random.randint(jax.random.fold_in(stream_key, axis), (), 0, shape[axis]) for axis in range(len(shape))]
    entries = entries.at[tuple(place)].set(low)
    longest = shape.index(max(shape))
    place[longest] = (place[longest] + 1) % shape[longest]
    return entries.at[tuple(place)].set(high)


def steps_of(rng, extent, cuts, low, top_value):
    level = 1.0
    for position, parts in cuts:
        heights = jax.random.uniform(jax.random.fold_in(jax.random.fold_in(rng, 6), position), (parts,), jnp.float32, low / len(cuts), top_value / len(cuts))
        level = level * jnp.repeat(jnp.exp(heights), extent[position] // parts).reshape((-1,) + (1,) * (len(extent) - 1 - position))
    return level


def shared_out(stream_key, own, number, rows, amount, top, bound, skew):
    ranking = jax.random.permutation(stream_key, amount)
    crowded, usual = load_shares(amount, rows * top, bound, skew, True), load_shares(amount, rows * top, bound, skew, False)
    places = jnp.arange(amount)

    def named(sizes, turn):
        used = int((sizes > 0).sum())
        fixed = max(1, used // 4)
        shifted = fixed + (places - fixed + turn * (used - fixed)) % max(1, amount - fixed)
        return jnp.zeros((amount,), jnp.int32).at[ranking[jnp.where(places < fixed, places, shifted)]].set(jnp.asarray(sizes, jnp.int32))

    sizes = jnp.where(number % 4 == 0, named(crowded, number // 4), named(usual, number - number // 4 - 1))
    mixed = jax.random.permutation(jax.random.fold_in(own, 3), amount)
    giver, sink = mixed[0:amount // 2 * 2:2], mixed[1:amount // 2 * 2:2]
    slack = jnp.minimum(sizes[giver] - 1, bound - sizes[sink]) // 2
    slack = jnp.where((giver == ranking[0]) | (sink == ranking[0]) | (sizes[sink] == 0), 0, jnp.maximum(slack, 0))
    shifted = jax.random.randint(jax.random.fold_in(own, 4), (amount // 2,), 0, 1 << 20) % (slack + 1)
    sizes = sizes.at[giver].add(-shifted).at[sink].add(shifted)
    members = jnp.searchsorted(jnp.cumsum(sizes), jnp.arange(rows * top), side="right").astype(jnp.int32)
    table = members.reshape(top, rows).T
    table = table[jax.random.permutation(jax.random.fold_in(own, 1), rows)]
    turn = jax.random.randint(jax.random.fold_in(own, 2), (rows, 1), 0, top)
    return jnp.take_along_axis(table, (jnp.arange(top)[None, :] + turn) % top, axis=1)


def load_shares(amount, total, most, lean, full):
    loads = [(1 << 20) // math.isqrt(rank ** lean) + 1 for rank in range(1, amount + 1)]
    largest = most if full else min(most, max(-(-total // amount), total * loads[0] // sum(loads)))
    least = 1 if total - largest >= amount - 1 else 0
    given, rest = [largest] + [least] * (amount - 1), total - largest - least * (amount - 1)
    while rest > 0:
        free = [i for i in range(1, amount) if given[i] < largest] or [i for i in range(1, amount) if given[i] < most]
        whole, remaining = sum([loads[i] for i in free]), rest
        for i in free:
            addition = min(most - given[i], max(1, remaining * loads[i] // whole), rest)
            given[i] = given[i] + addition
            rest = rest - addition
    return np.array(given)


def normal_values(stream_key, dims, deviation, most, cuts=(), kind=jnp.bfloat16):
    values = deviation * jax.random.normal(stream_key, dims, jnp.float32)
    if cuts:
        values = values * steps_of(stream_key, dims, cuts, -0.22, 0.18)
    return jnp.clip(values, -most, most).astype(kind)


def setup_inputs(seed: int = 0, part: int = 0) -> dict:
    seeds = jax.random.split(jax.random.key(seed), 11)
    part_keys = jax.random.split(jax.random.fold_in(seeds[10], part), 11)
    hidden_state = normal_values(part_keys[0], (STREAMS, D), 1.0, 6.0, ((0, 32),))
    cross_query = draw_cross_query(jax.random.fold_in(jax.random.fold_in(seeds[10], part), 71), part)
    source_keys = draw_source_keys(jax.random.fold_in(jax.random.fold_in(seeds[10], part), 71), part)
    source_values = normal_values(part_keys[3], (STREAMS, SRC, D), 1.0, 6.0, ((0, 32),))
    src_lengths = place_ends(jax.random.randint(part_keys[4], (STREAMS,), 2, SRC + 1), jax.random.fold_in(part_keys[4], 1), 2, SRC).astype(jnp.int32)
    norm_gain = jnp.clip(1.0 + 0.1 * jax.random.normal(seeds[5], (D,), jnp.float32), 0.5, 1.5)
    w_in = normal_values(seeds[6], (D, EXPERTS * FF), D ** -0.5, 0.125, ((1, 32),))
    w_out = normal_values(seeds[7], (EXPERTS * FF, D), FF ** -0.5, 0.09375, ((0, 32),))
    expert_ids_keys = jax.random.split(jax.random.fold_in(part_keys[8], 1), STREAMS // STREAMS_DEV)
    expert_ids_turns = jax.random.permutation(jax.random.fold_in(part_keys[8], 3), STREAMS // STREAMS_DEV)
    expert_ids = jax.vmap(lambda own, number: shared_out(jax.random.fold_in(part_keys[8], 2), own, number, STREAMS_DEV, EXPERTS, 2, CAP, 2))(expert_ids_keys, expert_ids_turns).reshape((STREAMS, 2))
    route_weights = jnp.clip(0.2 + 0.8 * jax.random.uniform(part_keys[9], (STREAMS, 2), jnp.float32) ** steps_of(part_keys[9], (STREAMS, 2), ((0, 32),), -0.2, 0.2), 0.2, 1.0)
    return dict(hidden_state=hidden_state, cross_query=cross_query, source_keys=source_keys, source_values=source_values, src_lengths=src_lengths, norm_gain=norm_gain, w_in=w_in, w_out=w_out, expert_ids=expert_ids, route_weights=route_weights)


def attend(block):
    queries, keys, values, lengths = block
    count = queries.shape[0]
    head_size = D // HEADS
    query_heads = queries.astype(jnp.float32).reshape(count, HEADS, head_size)
    key_heads = keys.astype(jnp.float32).reshape(count, SRC, HEADS, head_size)
    value_heads = values.astype(jnp.float32).reshape(count, SRC, HEADS, head_size)
    scores = jnp.einsum('bhd,bphd->bhp', query_heads, key_heads) / jnp.sqrt(jnp.float32(head_size))
    visible = jnp.arange(SRC, dtype=jnp.int32)[None, :] < lengths[:, None]
    scores = jnp.where(visible[:, None, :], scores, -1e+30)
    row_max = lax.optimization_barrier(jnp.max(scores, axis=-1, keepdims=True))
    expo = jnp.exp(scores - row_max)
    probabilities = (expo / lax.optimization_barrier(jnp.sum(expo, axis=-1, keepdims=True))).astype(jnp.bfloat16)
    probabilities = lax.optimization_barrier(probabilities).astype(jnp.float32)
    result = jnp.einsum('bhp,bphd->bhd', probabilities, value_heads)
    return result.reshape(count, D)

def reference(hidden_state, cross_query, source_keys, source_values, src_lengths, norm_gain, w_in, w_out, expert_ids, route_weights):
    blocks = (cross_query.reshape(N_EXPERT, STREAMS_DEV, D), source_keys.reshape(N_EXPERT, STREAMS_DEV, SRC, D), source_values.reshape(N_EXPERT, STREAMS_DEV, SRC, D), src_lengths.reshape(N_EXPERT, STREAMS_DEV))
    attended = lax.map(attend, blocks).reshape(STREAMS, D)
    mixed = hidden_state.astype(jnp.float32) + attended
    average = lax.optimization_barrier(jnp.mean(mixed, axis=-1, keepdims=True))
    centered = mixed - average
    variance = lax.optimization_barrier(jnp.mean(centered * centered, axis=-1, keepdims=True))
    normed = (centered * lax.rsqrt(variance + 1e-05) * norm_gain).astype(jnp.bfloat16)
    pairs = STREAMS * 2
    flat_ids = expert_ids.reshape(pairs).astype(jnp.int32)
    block_ids = flat_ids.reshape(N_EXPERT, 2 * STREAMS_DEV)
    onehot = (block_ids[:, :, None] == jnp.arange(EXPERTS, dtype=jnp.int32)[None, None, :]).astype(jnp.int32)
    slot_rank = lax.optimization_barrier(jnp.sum((jnp.cumsum(onehot, axis=1) - onehot) * onehot, axis=-1)).reshape(pairs)
    pair_index = jnp.arange(pairs, dtype=jnp.int32)
    slot_global = pair_index // (2 * STREAMS_DEV) * CAP + slot_rank
    table = jnp.full((EXPERTS, N_EXPERT * CAP), STREAMS, dtype=jnp.int32)
    table = table.at[flat_ids, slot_global].set(pair_index // 2)
    normed_pad = jnp.concatenate([normed, jnp.zeros((1, D), jnp.bfloat16)], axis=0)

    def run_expert(expert):
        rows = normed_pad[table[expert]]
        first = lax.dynamic_slice_in_dim(w_in, expert * FF, FF, 1)
        second = lax.dynamic_slice_in_dim(w_out, expert * FF, FF, 0)
        act = jnp.maximum(jnp.dot(rows, first, preferred_element_type=jnp.float32), 0.0).astype(jnp.bfloat16)
        return jnp.dot(act, second, preferred_element_type=jnp.float32)
    outputs = lax.map(run_expert, jnp.arange(EXPERTS, dtype=jnp.int32))
    flat_out = outputs.reshape(EXPERTS * N_EXPERT * CAP, D)
    pick = flat_ids * (N_EXPERT * CAP) + slot_global
    chosen = flat_out[pick].reshape(STREAMS, 2, D)
    moe = lax.optimization_barrier(jnp.sum(chosen * route_weights[:, :, None], axis=1))
    return (mixed + moe).astype(jnp.bfloat16)
```

```python
import jax
import jax.numpy as jnp
from jax import lax
from jax.sharding import PartitionSpec as P

HEADS = 16
SPLIT = 8
CORES = 2


def swap(value, distance, devices):
    pairs = [(source, source ^ distance) for source in range(devices)]
    return lax.ppermute(value, "expert", pairs)


def outer_groups(devices):
    return [list(range(inner, devices, SPLIT)) for inner in range(SPLIT)]


def to_experts(blocks, experts_count, devices):
    if experts_count > 4:
        stacked = jnp.stack(blocks)
        moved = lax.all_to_all(
            stacked,
            "expert",
            split_axis=0,
            concat_axis=0,
            tiled=True,
            axis_index_groups=outer_groups(devices),
        )
        return [moved[index] for index in range(experts_count)]
    return [
        block if distance == 0 else swap(block, distance * SPLIT, devices)
        for distance, block in enumerate(blocks)
    ]


def attend(hidden_state, cross_query, source_keys, source_values, src_lengths):
    streams, width = hidden_state.shape
    span = source_keys.shape[1]
    head_size = width // HEADS
    query_heads = cross_query.reshape(streams, HEADS, head_size)
    key_heads = source_keys.reshape(streams, span, HEADS, head_size)
    value_heads = source_values.reshape(streams, span, HEADS, head_size)
    scores = jnp.einsum("bhd,bphd->bhp", query_heads, key_heads, preferred_element_type=jnp.float32)
    scores = scores / jnp.sqrt(jnp.float32(head_size))
    visible = jnp.arange(span, dtype=jnp.int32)[None, :] < src_lengths[:, None]
    scores = jnp.where(visible[:, None, :], scores, -1e30)
    row_max = jnp.max(scores, axis=-1, keepdims=True)
    expo = jnp.exp(scores - row_max)
    probabilities = (expo / jnp.sum(expo, axis=-1, keepdims=True)).astype(jnp.bfloat16)
    attended = jnp.einsum(
        "bhp,bphd->bhd", probabilities, value_heads, preferred_element_type=jnp.float32
    )
    return hidden_state.astype(jnp.float32) + attended.reshape(streams, width)


def normalise(mixed, norm_gain):
    average = jnp.mean(mixed, axis=-1, keepdims=True)
    centered = mixed - average
    variance = jnp.mean(centered * centered, axis=-1, keepdims=True)
    return (centered * lax.rsqrt(variance + 1e-05) * norm_gain).astype(jnp.bfloat16)


def feed_forward(rows, w_in, w_out):
    act = jnp.maximum(jnp.dot(rows, w_in, preferred_element_type=jnp.float32), 0.0)
    return jnp.dot(act.astype(jnp.bfloat16), w_out, preferred_element_type=jnp.float32)


def on_device(
    hidden_state,
    cross_query,
    source_keys,
    source_values,
    src_lengths,
    norm_gain,
    w_in,
    w_out,
    expert_ids,
    route_weights,
):
    streams, width = hidden_state.shape
    devices = lax.axis_size("expert")
    experts_count = devices // SPLIT
    capacity = max(2, min(streams, 4 * streams * SPLIT // devices))
    direct = experts_count <= 4
    mixed = attend(hidden_state, cross_query, source_keys, source_values, src_lengths)
    normed = normalise(mixed, norm_gain)
    group = lax.axis_index("expert") // SPLIT
    order = jnp.arange(experts_count, dtype=jnp.int32)
    if direct:
        order = order ^ group
    chosen = expert_ids[:, :, None] == order[None, None, :]
    weights = jnp.sum(jnp.where(chosen, route_weights[:, :, None], 0.0), axis=1)
    if capacity >= streams:
        blocks = [normed] * experts_count
    else:
        named = jnp.any(chosen, axis=1).astype(jnp.int32)
        rank = jnp.cumsum(named, axis=0) - named
        slots = jnp.arange(capacity, dtype=jnp.int32)
        placed = (named == 1)[None, :, :] & (rank[None, :, :] == slots[:, None, None])
        packed = jnp.einsum(
            "ctk,td->kcd",
            placed.astype(jnp.bfloat16),
            normed,
            preferred_element_type=jnp.float32,
        ).astype(jnp.bfloat16)
        blocks = [packed[index] for index in range(experts_count)]
    arrived = jnp.concatenate(to_experts(blocks, experts_count, devices), axis=0)
    column = arrived.shape[0]
    chips = SPLIT // CORES
    near = [arrived] + [swap(arrived, CORES * step, devices) for step in range(1, chips)]
    near = jnp.concatenate(near, axis=0)
    far = swap(near, 1, devices)
    out_far = feed_forward(far, w_in, w_out)
    out_near = feed_forward(near, w_in, w_out)
    out_near = out_near + swap(out_far.astype(jnp.bfloat16), 1, devices).astype(jnp.float32)
    parts = out_near.reshape(chips, column, width)
    total = parts[0]
    for step in range(1, chips):
        total = total + swap(parts[step].astype(jnp.bfloat16), CORES * step, devices).astype(
            jnp.float32
        )
    total = total.reshape(experts_count, capacity, width)
    result = mixed
    sent = total.astype(jnp.bfloat16)
    returned = to_experts([sent[k] for k in range(experts_count)], experts_count, devices)
    for k in range(experts_count):
        part = total[0] if direct and k == 0 else returned[k].astype(jnp.float32)
        if capacity < streams:
            part = jnp.einsum(
                "ct,cd->td",
                placed[:, :, k].astype(jnp.float32),
                part,
                precision=lax.Precision.HIGHEST,
                preferred_element_type=jnp.float32,
            )
        result = result + weights[:, k : k + 1] * part
    return result.astype(jnp.bfloat16)


def solution(mesh):
    placed = (
        P(("group", "expert"), None),
        P(("group", "expert"), None),
        P(("group", "expert"), None, None),
        P(("group", "expert"), None, None),
        P(("group", "expert")),
        P(),
        P(None, "expert"),
        P("expert", None),
        P(("group", "expert"), None),
        P(("group", "expert"), None),
    )
    return jax.shard_map(
        on_device,
        mesh=mesh,
        in_specs=placed,
        out_specs=P(("group", "expert"), None),
        check_vma=False,
    )
```

```python
import jax
import jax.numpy as jnp
from jax import lax
from jax.experimental import pallas as pl
from jax.experimental.pallas import tpu as pltpu
from jax.sharding import PartitionSpec as P

HEADS = 16
SPLIT = 8
CORES = 2
PIECES = 4


def swap(value, distance, devices):
    pairs = [(source, source ^ distance) for source in range(devices)]
    return lax.ppermute(value, "expert", pairs)


def outer_groups(devices):
    return [list(range(inner, devices, SPLIT)) for inner in range(SPLIT)]


def to_experts(blocks, experts_count, devices):
    if experts_count > 4:
        stacked = jnp.stack(blocks)
        moved = lax.all_to_all(
            stacked,
            "expert",
            split_axis=0,
            concat_axis=0,
            tiled=True,
            axis_index_groups=outer_groups(devices),
        )
        return [moved[index] for index in range(experts_count)]
    return [
        block if distance == 0 else swap(block, distance * SPLIT, devices)
        for distance, block in enumerate(blocks)
    ]


def attend_kernel(lengths_in, hidden_in, query_in, keys, values, gain_in, mixed, normed, lengths, hidden, query, gain, key_buf, value_buf, score_buf, small_sem, key_sem, value_sem):
    streams, width = hidden.shape
    span = key_buf.shape[1]
    head_size = width // HEADS
    group = key_buf.shape[0] // PIECES
    small = [
        pltpu.make_async_copy(query_in, query, small_sem.at[0]),
        pltpu.make_async_copy(lengths_in, lengths, small_sem.at[1]),
        pltpu.make_async_copy(hidden_in, hidden, small_sem.at[2]),
        pltpu.make_async_copy(gain_in, gain, small_sem.at[3]),
    ]
    pieces = [pl.ds(piece * group, group) for piece in range(PIECES)]
    key_copies = [pltpu.make_async_copy(keys.at[p], key_buf.at[p], key_sem.at[i]) for i, p in enumerate(pieces)]
    value_copies = [pltpu.make_async_copy(values.at[p], value_buf.at[p], value_sem.at[i]) for i, p in enumerate(pieces)]
    for copy in small + key_copies + value_copies:
        copy.start()
    owner = lax.broadcasted_iota(jnp.int32, (HEADS, width), 1) // head_size
    own = owner == lax.broadcasted_iota(jnp.int32, (HEADS, width), 0)
    position = lax.broadcasted_iota(jnp.int32, (HEADS, span), 1)
    small[0].wait()
    small[1].wait()
    for b in range(streams):
        if b % group == 0:
            key_copies[b // group].wait()
        spread = jnp.where(own, query[b : b + 1, :].astype(jnp.float32), 0.0).astype(jnp.bfloat16)
        scores = lax.dot_general(spread, key_buf[b], (((1,), (1,)), ((), ())), preferred_element_type=jnp.float32)
        scores = scores / jnp.sqrt(jnp.float32(head_size))
        score_buf[b * HEADS : (b + 1) * HEADS, :] = jnp.where(position < lengths[b], scores, -1e30)
    scores = score_buf[...]
    expo = jnp.exp(scores - jnp.max(scores, axis=-1, keepdims=True))
    score_buf[...] = expo / jnp.sum(expo, axis=-1, keepdims=True)
    for b in range(streams):
        if b % group == 0:
            value_copies[b // group].wait()
        probabilities = score_buf[b * HEADS : (b + 1) * HEADS, :].astype(jnp.bfloat16)
        every = jnp.dot(probabilities, value_buf[b], preferred_element_type=jnp.float32)
        for h in range(HEADS):
            lanes = slice(h * head_size, (h + 1) * head_size)
            mixed[b : b + 1, lanes] = every[h : h + 1, lanes]
    small[2].wait()
    small[3].wait()
    total = hidden[...].astype(jnp.float32) + mixed[...]
    mixed[...] = total
    centered = total - jnp.mean(total, axis=-1, keepdims=True)
    variance = jnp.mean(centered * centered, axis=-1, keepdims=True)
    normed[...] = (centered * lax.rsqrt(variance + 1e-05) * gain[...]).astype(jnp.bfloat16)
def attend(hidden_state, cross_query, source_keys, source_values, src_lengths, norm_gain):
    streams, width = hidden_state.shape
    span = source_keys.shape[1]
    vmem = pl.BlockSpec(memory_space=pltpu.VMEM)
    hbm = pl.BlockSpec(memory_space=pl.ANY)
    return pl.pallas_call(
        attend_kernel,
        out_shape=(jax.ShapeDtypeStruct((streams, width), jnp.float32), jax.ShapeDtypeStruct((streams, width), jnp.bfloat16)),
        in_specs=[hbm]*6,
        out_specs=(vmem, vmem),
        scratch_shapes=[
            pltpu.SMEM((streams,), jnp.int32),
            pltpu.VMEM((streams, width), hidden_state.dtype),
            pltpu.VMEM((streams, width), cross_query.dtype),
            pltpu.VMEM((1, width), norm_gain.dtype),
            pltpu.VMEM((streams, span, width), source_keys.dtype),
            pltpu.VMEM((streams, span, width), source_values.dtype),
            pltpu.VMEM((streams * HEADS, span), jnp.float32),
            pltpu.SemaphoreType.DMA((4,)),
            pltpu.SemaphoreType.DMA((PIECES,)),
            pltpu.SemaphoreType.DMA((PIECES,)),
        ],
    )(src_lengths, hidden_state, cross_query, source_keys, source_values, norm_gain.reshape(1, width))


def on_device(
    hidden_state,
    cross_query,
    source_keys,
    source_values,
    src_lengths,
    norm_gain,
    w_in,
    w_out,
    expert_ids,
    route_weights,
):
    streams, width = hidden_state.shape
    devices = lax.axis_size("expert")
    experts_count = devices // SPLIT
    capacity = max(2, min(streams, 4 * streams * SPLIT // devices))
    direct = experts_count <= 4
    mixed, normed = attend(
        hidden_state, cross_query, source_keys, source_values, src_lengths, norm_gain
    )
    group = lax.axis_index("expert") // SPLIT
    order = jnp.arange(experts_count, dtype=jnp.int32)
    if direct:
        order = order ^ group
    chosen = expert_ids[:, :, None] == order[None, None, :]
    weights = jnp.sum(jnp.where(chosen, route_weights[:, :, None], 0.0), axis=1)
    if capacity >= streams:
        blocks = [normed] * experts_count
    else:
        named = jnp.any(chosen, axis=1).astype(jnp.int32)
        rank = jnp.cumsum(named, axis=0) - named
        slots = jnp.arange(capacity, dtype=jnp.int32)
        placed = (named == 1)[None, :, :] & (rank[None, :, :] == slots[:, None, None])
        packed = jnp.einsum(
            "ctk,td->kcd",
            placed.astype(jnp.bfloat16),
            normed,
            preferred_element_type=jnp.float32,
        ).astype(jnp.bfloat16)
        blocks = [packed[index] for index in range(experts_count)]
    arrived = jnp.concatenate(to_experts(blocks, experts_count, devices), axis=0)
    column = arrived.shape[0]
    chips = SPLIT // CORES
    near = [arrived] + [swap(arrived, CORES * step, devices) for step in range(1, chips)]
    near = jnp.concatenate(near, axis=0)
    far = swap(near, 1, devices)
    rows = jnp.concatenate([far, near], axis=0)
    act = jnp.maximum(jnp.dot(rows, w_in, preferred_element_type=jnp.float32), 0.0)
    act = act.astype(jnp.bfloat16)
    half = near.shape[0]
    out_far = jnp.dot(act[:half], w_out, preferred_element_type=jnp.float32)
    given = swap(out_far.astype(jnp.bfloat16), 1, devices)
    out_near = jnp.dot(act[half:], w_out, preferred_element_type=jnp.float32)
    out_near = out_near + given.astype(jnp.float32)
    parts = out_near.reshape(chips, column, width)
    total = parts[0]
    for step in range(1, chips):
        total = total + swap(parts[step].astype(jnp.bfloat16), CORES * step, devices).astype(
            jnp.float32
        )
    total = total.reshape(experts_count, capacity, width)
    result = mixed
    sent = total.astype(jnp.bfloat16)
    returned = to_experts([sent[k] for k in range(experts_count)], experts_count, devices)
    for k in range(experts_count):
        part = total[0] if direct and k == 0 else returned[k].astype(jnp.float32)
        if capacity < streams:
            part = jnp.einsum(
                "ct,cd->td",
                placed[:, :, k].astype(jnp.float32),
                part,
                precision=lax.Precision.HIGHEST,
                preferred_element_type=jnp.float32,
            )
        result = result + weights[:, k : k + 1] * part
    return result.astype(jnp.bfloat16)


def solution(mesh):
    placed = (
        P(("group", "expert"), None),
        P(("group", "expert"), None),
        P(("group", "expert"), None, None),
        P(("group", "expert"), None, None),
        P(("group", "expert")),
        P(),
        P(None, "expert"),
        P("expert", None),
        P(("group", "expert"), None),
        P(("group", "expert"), None),
    )
    return jax.shard_map(
        on_device,
        mesh=mesh,
        in_specs=placed,
        out_specs=P(("group", "expert"), None),
        check_vma=False,
    )
```

```python
import jax
import jax.numpy as jnp
from jax import lax
from jax.experimental import pallas as pl
from jax.experimental.pallas import tpu as pltpu
from jax.sharding import PartitionSpec as P

HEADS = 16
SPLIT = 8
CORES = 2
PIECES = 4
VMEM_LIMIT = 16 * 1024 * 1024


def swap(value, distance, devices):
    pairs = [(source, source ^ distance) for source in range(devices)]
    return lax.ppermute(value, "expert", pairs)


def outer_exchange(blocks, devices):
    moved = lax.all_to_all(
        jnp.stack(blocks),
        "expert",
        split_axis=0,
        concat_axis=0,
        tiled=True,
        axis_index_groups=[list(range(inner, devices, SPLIT)) for inner in range(SPLIT)],
    )
    return [moved[index] for index in range(len(blocks))]


def far_first(count):
    return list(range(count - 1, 0, -1))


def attend_kernel(lengths_in, hidden_in, query_in, keys, values, gain_in, mixed, normed, lengths, hidden, query, gain, key_buf, value_buf, score_buf, small_sem, key_sem, value_sem):
    streams, width = hidden.shape
    span = key_buf.shape[1]
    head_size = width // HEADS
    group = key_buf.shape[0] // PIECES
    small = [
        pltpu.make_async_copy(query_in, query, small_sem.at[0]),
        pltpu.make_async_copy(lengths_in, lengths, small_sem.at[1]),
        pltpu.make_async_copy(hidden_in, hidden, small_sem.at[2]),
        pltpu.make_async_copy(gain_in, gain, small_sem.at[3]),
    ]
    pieces = [pl.ds(piece * group, group) for piece in range(PIECES)]
    key_copies = [pltpu.make_async_copy(keys.at[p], key_buf.at[p], key_sem.at[i]) for i, p in enumerate(pieces)]
    value_copies = [pltpu.make_async_copy(values.at[p], value_buf.at[p], value_sem.at[i]) for i, p in enumerate(pieces)]
    for copy in small + key_copies + value_copies:
        copy.start()
    owner = lax.broadcasted_iota(jnp.int32, (HEADS, width), 1) // head_size
    own = owner == lax.broadcasted_iota(jnp.int32, (HEADS, width), 0)
    position = lax.broadcasted_iota(jnp.int32, (HEADS, span), 1)
    small[0].wait()
    small[1].wait()
    for b in range(streams):
        if b % group == 0:
            key_copies[b // group].wait()
        spread = jnp.where(own, query[b : b + 1, :].astype(jnp.float32), 0.0).astype(jnp.bfloat16)
        scores = lax.dot_general(spread, key_buf[b], (((1,), (1,)), ((), ())), preferred_element_type=jnp.float32)
        scores = scores / jnp.sqrt(jnp.float32(head_size))
        score_buf[b * HEADS : (b + 1) * HEADS, :] = jnp.where(position < lengths[b], scores, -1e30)
    scores = score_buf[...]
    expo = jnp.exp(scores - jnp.max(scores, axis=-1, keepdims=True))
    score_buf[...] = expo / jnp.sum(expo, axis=-1, keepdims=True)
    for b in range(streams):
        if b % group == 0:
            value_copies[b // group].wait()
        probabilities = score_buf[b * HEADS : (b + 1) * HEADS, :].astype(jnp.bfloat16)
        every = jnp.dot(probabilities, value_buf[b], preferred_element_type=jnp.float32)
        for h in range(HEADS):
            lanes = slice(h * head_size, (h + 1) * head_size)
            mixed[b : b + 1, lanes] = every[h : h + 1, lanes]
    small[2].wait()
    small[3].wait()
    total = hidden[...].astype(jnp.float32) + mixed[...]
    mixed[...] = total
    centered = total - jnp.mean(total, axis=-1, keepdims=True)
    variance = jnp.mean(centered * centered, axis=-1, keepdims=True)
    normed[...] = (centered * lax.rsqrt(variance + 1e-05) * gain[...]).astype(jnp.bfloat16)


def attend(hidden_state, cross_query, source_keys, source_values, src_lengths, norm_gain):
    streams, width = hidden_state.shape
    span = source_keys.shape[1]
    arrays = (
        src_lengths,
        hidden_state,
        cross_query,
        source_keys,
        source_values,
        norm_gain.reshape(1, width),
    )
    vmem = pl.BlockSpec(memory_space=pltpu.VMEM)
    hbm = pl.BlockSpec(memory_space=pltpu.HBM)
    return pl.pallas_call(
        attend_kernel,
        out_shape=(jax.ShapeDtypeStruct((streams, width), jnp.float32), jax.ShapeDtypeStruct((streams, width), jnp.bfloat16)),
        in_specs=[hbm]*6,
        out_specs=(vmem, vmem),
        scratch_shapes=[
            pltpu.SMEM((streams,), jnp.int32),
            pltpu.VMEM((streams, width), hidden_state.dtype),
            pltpu.VMEM((streams, width), cross_query.dtype),
            pltpu.VMEM((1, width), norm_gain.dtype),
            pltpu.VMEM((streams, span, width), source_keys.dtype),
            pltpu.VMEM((streams, span, width), source_values.dtype),
            pltpu.VMEM((streams * HEADS, span), jnp.float32),
            pltpu.SemaphoreType.DMA((4,)),
            pltpu.SemaphoreType.DMA((PIECES,)),
            pltpu.SemaphoreType.DMA((PIECES,)),
        ],
        compiler_params=pltpu.CompilerParams(vmem_limit_bytes=VMEM_LIMIT),
    )(*[pltpu.with_memory_space_constraint(array, pltpu.HBM) for array in arrays])


def step_on_device(
    hidden_state,
    cross_query,
    source_keys,
    source_values,
    src_lengths,
    norm_gain,
    w_in,
    w_out,
    expert_ids,
    route_weights,
):
    streams, width = hidden_state.shape
    devices = lax.axis_size("expert")
    experts_count = devices // SPLIT
    capacity = max(2, min(streams, 4 * streams * SPLIT // devices))
    direct = experts_count <= 4
    mixed, normed = attend(
        hidden_state, cross_query, source_keys, source_values, src_lengths, norm_gain
    )
    group = lax.axis_index("expert") // SPLIT
    order = jnp.arange(experts_count, dtype=jnp.int32)
    if direct:
        order = order ^ group
    chosen = expert_ids[:, :, None] == order[None, None, :]
    weights = jnp.sum(jnp.where(chosen, route_weights[:, :, None], 0.0), axis=1)
    if capacity >= streams:
        blocks = [normed] * experts_count
    else:
        named = jnp.any(chosen, axis=1).astype(jnp.int32)
        rank = jnp.cumsum(named, axis=0) - named
        slots = jnp.arange(capacity, dtype=jnp.int32)
        placed = (named == 1)[None, :, :] & (rank[None, :, :] == slots[:, None, None])
        packed = jnp.einsum(
            "ctk,td->kcd",
            placed.astype(jnp.bfloat16),
            normed,
            preferred_element_type=jnp.float32,
        ).astype(jnp.bfloat16)
        blocks = [packed[index] for index in range(experts_count)]
    chips = SPLIT // CORES
    steps = far_first(chips)
    distances = far_first(experts_count)
    if direct:
        planes = {k: swap(blocks[k], k * SPLIT, devices) for k in distances}
        first = [blocks[0]]
        rest = [planes[k] for k in range(1, experts_count)]
    else:
        first = outer_exchange(blocks, devices)
        rest = []
    first, *others = [jnp.concatenate(part, axis=0) for part in (first, rest) if part]
    near = {0: [first] + others}
    early = {step: swap(first, CORES * step, devices) for step in steps}
    late = {step: [swap(part, CORES * step, devices) for part in others] for step in steps}
    for step in steps:
        near[step] = [early[step]] + late[step]
    far = {step: [swap(part, 1, devices) for part in near[step]] for step in range(chips)}
    order = [(step, place) for step in range(chips) for place in range(1 + len(others))]

    spans = {}
    count = 0
    for step, place in order:
        spans[step, place] = (count, near[step][place].shape[0])
        count += near[step][place].shape[0]
    rows = [near[step][place] for step, place in order] + [far[step][place] for step, place in order]
    units = jnp.dot(jnp.concatenate(rows, axis=0), w_in, preferred_element_type=jnp.float32)
    act = lax.optimization_barrier(jnp.maximum(units, 0.0).astype(jnp.bfloat16))
    far_sent = jnp.dot(act[count:], w_out, preferred_element_type=jnp.float32).astype(jnp.bfloat16)
    near_every = jnp.dot(act[:count], w_out, preferred_element_type=jnp.float32)
    near_every = lax.optimization_barrier(near_every)

    def of(every, step, place):
        start, length = spans[step, place]
        return every[start : start + length]

    pair = {
        (step, place): of(near_every, step, place)
        + swap(of(far_sent, step, place), 1, devices).astype(jnp.float32)
        for step, place in order
    }

    def chip_sum(place):
        total = pair[0, place]
        for step in steps:
            sent = pair[step, place].astype(jnp.bfloat16)
            total = total + swap(sent, CORES * step, devices).astype(jnp.float32)
        return total

    result = mixed
    if direct:
        away = chip_sum(1).reshape(experts_count - 1, capacity, width)
        back = {k: swap(away[k - 1].astype(jnp.bfloat16), k * SPLIT, devices) for k in distances}
        own = chip_sum(0)
        parts = [own] + [back[k].astype(jnp.float32) for k in range(1, experts_count)]
    else:
        total = chip_sum(0).astype(jnp.bfloat16)
        total = total.reshape(experts_count, capacity, width)
        back = outer_exchange([total[k] for k in range(experts_count)], devices)
        parts = [part.astype(jnp.float32) for part in back]
    for k, part in enumerate(parts):
        if capacity < streams:
            part = jnp.einsum(
                "ct,cd->td",
                placed[:, :, k].astype(jnp.float32),
                part,
                precision=lax.Precision.HIGHEST,
                preferred_element_type=jnp.float32,
            )
        result = result + weights[:, k : k + 1] * part
    return result.astype(jnp.bfloat16)


def solution(mesh):
    placed = (
        P(("group", "expert"), None),
        P(("group", "expert"), None),
        P(("group", "expert"), None, None),
        P(("group", "expert"), None, None),
        P(("group", "expert")),
        P(),
        P(None, "expert"),
        P("expert", None),
        P(("group", "expert"), None),
        P(("group", "expert"), None),
    )
    return jax.shard_map(
        step_on_device,
        mesh=mesh,
        in_specs=placed,
        out_specs=P(("group", "expert"), None),
        check_vma=False,
    )
```

```python
import jax
import jax.numpy as jnp
from jax import lax
from jax.experimental import pallas as pl
from jax.experimental.pallas import tpu as pltpu
from jax.sharding import PartitionSpec as P

HEADS = 16
SPLIT = 8
CORES = 2
PIECES = 4
VMEM_LIMIT = 16 * 1024 * 1024


def swap(value, distance, devices):
    pairs = [(source, source ^ distance) for source in range(devices)]
    return lax.ppermute(value, "expert", pairs)


def outer_exchange(blocks, devices):
    moved = lax.all_to_all(
        jnp.stack(blocks),
        "expert",
        split_axis=0,
        concat_axis=0,
        tiled=True,
        axis_index_groups=[list(range(inner, devices, SPLIT)) for inner in range(SPLIT)],
    )
    return [moved[index] for index in range(len(blocks))]


def far_first(count):
    return list(range(count - 1, 0, -1))


def attend_kernel(lengths_in, hidden_in, query_in, keys, values, gain_in, mixed, normed, lengths, hidden, query, gain, key_buf, value_buf, score_buf, small_sem, key_sem, value_sem):
    streams, width = hidden.shape
    span = key_buf.shape[1]
    head_size = width // HEADS
    group = key_buf.shape[0] // PIECES
    small = [
        pltpu.make_async_copy(query_in, query, small_sem.at[0]),
        pltpu.make_async_copy(lengths_in, lengths, small_sem.at[1]),
        pltpu.make_async_copy(hidden_in, hidden, small_sem.at[2]),
        pltpu.make_async_copy(gain_in, gain, small_sem.at[3]),
    ]
    pieces = [pl.ds(piece * group, group) for piece in range(PIECES)]
    key_copies = [pltpu.make_async_copy(keys.at[p], key_buf.at[p], key_sem.at[i]) for i, p in enumerate(pieces)]
    value_copies = [pltpu.make_async_copy(values.at[p], value_buf.at[p], value_sem.at[i]) for i, p in enumerate(pieces)]
    for copy in small + key_copies + value_copies:
        copy.start()
    owner = lax.broadcasted_iota(jnp.int32, (HEADS, width), 1) // head_size
    own = owner == lax.broadcasted_iota(jnp.int32, (HEADS, width), 0)
    position = lax.broadcasted_iota(jnp.int32, (HEADS, span), 1)
    small[0].wait()
    small[1].wait()
    for b in range(streams):
        if b % group == 0:
            key_copies[b // group].wait()
        spread = jnp.where(own, query[b : b + 1, :].astype(jnp.float32), 0.0).astype(jnp.bfloat16)
        scores = lax.dot_general(spread, key_buf[b], (((1,), (1,)), ((), ())), preferred_element_type=jnp.float32)
        scores = scores / jnp.sqrt(jnp.float32(head_size))
        score_buf[b * HEADS : (b + 1) * HEADS, :] = jnp.where(position < lengths[b], scores, -1e30)
    scores = score_buf[...]
    expo = jnp.exp(scores - jnp.max(scores, axis=-1, keepdims=True))
    score_buf[...] = expo / jnp.sum(expo, axis=-1, keepdims=True)
    for b in range(streams):
        if b % group == 0:
            value_copies[b // group].wait()
        probabilities = score_buf[b * HEADS : (b + 1) * HEADS, :].astype(jnp.bfloat16)
        every = jnp.dot(probabilities, value_buf[b], preferred_element_type=jnp.float32)
        for h in range(HEADS):
            lanes = slice(h * head_size, (h + 1) * head_size)
            mixed[b : b + 1, lanes] = every[h : h + 1, lanes]
    small[2].wait()
    small[3].wait()
    total = hidden[...].astype(jnp.float32) + mixed[...]
    mixed[...] = total
    centered = total - jnp.mean(total, axis=-1, keepdims=True)
    variance = jnp.mean(centered * centered, axis=-1, keepdims=True)
    normed[...] = (centered * lax.rsqrt(variance + 1e-05) * gain[...]).astype(jnp.bfloat16)


def attend(hidden_state, cross_query, source_keys, source_values, src_lengths, norm_gain):
    streams, width = hidden_state.shape
    span = source_keys.shape[1]
    arrays = (
        src_lengths,
        hidden_state,
        cross_query,
        source_keys,
        source_values,
        norm_gain.reshape(1, width),
    )
    vmem = pl.BlockSpec(memory_space=pltpu.VMEM)
    hbm = pl.BlockSpec(memory_space=pltpu.HBM)
    return pl.pallas_call(
        attend_kernel,
        out_shape=(jax.ShapeDtypeStruct((streams, width), jnp.float32), jax.ShapeDtypeStruct((streams, width), jnp.bfloat16)),
        in_specs=[hbm]*6,
        out_specs=(vmem, vmem),
        scratch_shapes=[
            pltpu.SMEM((streams,), jnp.int32),
            pltpu.VMEM((streams, width), hidden_state.dtype),
            pltpu.VMEM((streams, width), cross_query.dtype),
            pltpu.VMEM((1, width), norm_gain.dtype),
            pltpu.VMEM((streams, span, width), source_keys.dtype),
            pltpu.VMEM((streams, span, width), source_values.dtype),
            pltpu.VMEM((streams * HEADS, span), jnp.float32),
            pltpu.SemaphoreType.DMA((4,)),
            pltpu.SemaphoreType.DMA((PIECES,)),
            pltpu.SemaphoreType.DMA((PIECES,)),
        ],
        compiler_params=pltpu.CompilerParams(vmem_limit_bytes=VMEM_LIMIT),
    )(*[pltpu.with_memory_space_constraint(array, pltpu.HBM) for array in arrays])


def step_on_device(
    hidden_state,
    cross_query,
    source_keys,
    source_values,
    src_lengths,
    norm_gain,
    w_in,
    w_out,
    expert_ids,
    route_weights,
):
    streams, width = hidden_state.shape
    devices = lax.axis_size("expert")
    experts_count = devices // SPLIT
    capacity = max(2, min(streams, 4 * streams * SPLIT // devices))
    direct = experts_count <= 4
    mixed, normed = attend(
        hidden_state, cross_query, source_keys, source_values, src_lengths, norm_gain
    )
    group = lax.axis_index("expert") // SPLIT
    order = jnp.arange(experts_count, dtype=jnp.int32)
    if direct:
        order = order ^ group
    chosen = expert_ids[:, :, None] == order[None, None, :]
    weights = jnp.sum(jnp.where(chosen, route_weights[:, :, None], 0.0), axis=1)
    if capacity >= streams:
        blocks = [normed] * experts_count
    else:
        named = jnp.any(chosen, axis=1).astype(jnp.int32)
        rank = jnp.cumsum(named, axis=0) - named
        slots = jnp.arange(capacity, dtype=jnp.int32)
        placed = (named == 1)[None, :, :] & (rank[None, :, :] == slots[:, None, None])
        packed = jnp.einsum(
            "ctk,td->kcd",
            placed.astype(jnp.bfloat16),
            normed,
            preferred_element_type=jnp.float32,
        ).astype(jnp.bfloat16)
        blocks = [packed[index] for index in range(experts_count)]
    chips = SPLIT // CORES
    steps = far_first(chips)
    distances = far_first(experts_count)
    if direct:
        planes = {k: swap(blocks[k], k * SPLIT, devices) for k in distances}
        column = [blocks[0]] + [planes[k] for k in range(1, experts_count)]
    else:
        column = outer_exchange(blocks, devices)
    near = {0: jnp.concatenate(column, axis=0)}
    count = near[0].shape[0]
    for step in range(1, chips):
        near[step] = swap(near[0], CORES * step, devices)
    far = {step: swap(near[step], 1, devices) for step in range(chips)}
    rows = [near[step] for step in range(chips)] + [far[step] for step in range(chips)]
    half = chips * count
    units = jnp.dot(jnp.concatenate(rows, axis=0), w_in, preferred_element_type=jnp.float32)
    act = lax.optimization_barrier(jnp.maximum(units, 0.0).astype(jnp.bfloat16))
    far_sent = jnp.dot(act[half:], w_out, preferred_element_type=jnp.float32).astype(jnp.bfloat16)
    near_every = jnp.dot(act[:half], w_out, preferred_element_type=jnp.float32)
    near_every = lax.optimization_barrier(near_every)
    pair = {}
    for step in steps + [0]:
        place = slice(step * count, (step + 1) * count)
        given = swap(far_sent[place], 1, devices)
        pair[step] = near_every[place] + given.astype(jnp.float32)
    total = pair[0]
    for step in steps:
        sent = pair[step].astype(jnp.bfloat16)
        total = total + swap(sent, CORES * step, devices).astype(jnp.float32)
    total = total.reshape(experts_count, capacity, width)
    result = mixed
    sent = total.astype(jnp.bfloat16)
    if direct:
        back = {k: swap(sent[k], k * SPLIT, devices) for k in distances}
        parts = [total[0]] + [back[k].astype(jnp.float32) for k in range(1, experts_count)]
    else:
        back = outer_exchange([sent[k] for k in range(experts_count)], devices)
        parts = [part.astype(jnp.float32) for part in back]
    for k, part in enumerate(parts):
        if capacity < streams:
            part = jnp.einsum(
                "ct,cd->td",
                placed[:, :, k].astype(jnp.float32),
                part,
                precision=lax.Precision.HIGHEST,
                preferred_element_type=jnp.float32,
            )
        result = result + weights[:, k : k + 1] * part
    return result.astype(jnp.bfloat16)


def solution(mesh):
    placed = (
        P(("group", "expert"), None),
        P(("group", "expert"), None),
        P(("group", "expert"), None, None),
        P(("group", "expert"), None, None),
        P(("group", "expert")),
        P(),
        P(None, "expert"),
        P("expert", None),
        P(("group", "expert"), None),
        P(("group", "expert"), None),
    )
    return jax.shard_map(
        step_on_device,
        mesh=mesh,
        in_specs=placed,
        out_specs=P(("group", "expert"), None),
        check_vma=False,
    )
```

```python
import jax
import jax.numpy as jnp
from jax import lax
from jax.experimental import pallas as pl
from jax.experimental.pallas import tpu as pltpu
from jax.sharding import PartitionSpec as P

HEADS = 16
SPLIT = 8
CORES = 2
PIECES = 4
VMEM_LIMIT = 16 * 1024 * 1024


def swap(value, distance, devices):
    pairs = [(source, source ^ distance) for source in range(devices)]
    return lax.ppermute(value, "expert", pairs)


def outer_exchange(blocks, devices):
    moved = lax.all_to_all(
        jnp.stack(blocks),
        "expert",
        split_axis=0,
        concat_axis=0,
        tiled=True,
        axis_index_groups=[list(range(inner, devices, SPLIT)) for inner in range(SPLIT)],
    )
    return [moved[index] for index in range(len(blocks))]


def far_first(count):
    return list(range(count - 1, 0, -1))


def attend_kernel(lengths_in, hidden_in, query_in, keys, values, gain_in, w_in_from, w_out_from, mixed, normed, w_in, w_out, lengths, hidden, query, gain, key_buf, value_buf, score_buf, small_sem, key_sem, value_sem):
    streams, width = hidden.shape
    span = key_buf.shape[1]
    head_size = width // HEADS
    group = key_buf.shape[0] // PIECES
    small = [
        pltpu.make_async_copy(query_in, query, small_sem.at[0]),
        pltpu.make_async_copy(lengths_in, lengths, small_sem.at[1]),
        pltpu.make_async_copy(hidden_in, hidden, small_sem.at[2]),
        pltpu.make_async_copy(gain_in, gain, small_sem.at[3]),
    ]
    pieces = [pl.ds(piece * group, group) for piece in range(PIECES)]
    key_copies = [pltpu.make_async_copy(keys.at[p], key_buf.at[p], key_sem.at[i]) for i, p in enumerate(pieces)]
    value_copies = [pltpu.make_async_copy(values.at[p], value_buf.at[p], value_sem.at[i]) for i, p in enumerate(pieces)]
    weights = [
        pltpu.make_async_copy(w_in_from, w_in, small_sem.at[4]),
        pltpu.make_async_copy(w_out_from, w_out, small_sem.at[5]),
    ]
    for copy in small + key_copies + value_copies + weights:
        copy.start()
    owner = lax.broadcasted_iota(jnp.int32, (HEADS, width), 1) // head_size
    own = owner == lax.broadcasted_iota(jnp.int32, (HEADS, width), 0)
    position = lax.broadcasted_iota(jnp.int32, (HEADS, span), 1)
    small[0].wait()
    small[1].wait()
    for b in range(streams):
        if b % group == 0:
            key_copies[b // group].wait()
        spread = jnp.where(own, query[b : b + 1, :].astype(jnp.float32), 0.0).astype(jnp.bfloat16)
        scores = lax.dot_general(spread, key_buf[b], (((1,), (1,)), ((), ())), preferred_element_type=jnp.float32)
        scores = scores / jnp.sqrt(jnp.float32(head_size))
        score_buf[b * HEADS : (b + 1) * HEADS, :] = jnp.where(position < lengths[b], scores, -1e30)
    scores = score_buf[...]
    expo = jnp.exp(scores - jnp.max(scores, axis=-1, keepdims=True))
    score_buf[...] = expo / jnp.sum(expo, axis=-1, keepdims=True)
    for b in range(streams):
        if b % group == 0:
            value_copies[b // group].wait()
        probabilities = score_buf[b * HEADS : (b + 1) * HEADS, :].astype(jnp.bfloat16)
        every = jnp.dot(probabilities, value_buf[b], preferred_element_type=jnp.float32)
        for h in range(HEADS):
            lanes = slice(h * head_size, (h + 1) * head_size)
            mixed[b : b + 1, lanes] = every[h : h + 1, lanes]
    small[2].wait()
    small[3].wait()
    total = hidden[...].astype(jnp.float32) + mixed[...]
    mixed[...] = total
    centered = total - jnp.mean(total, axis=-1, keepdims=True)
    variance = jnp.mean(centered * centered, axis=-1, keepdims=True)
    normed[...] = (centered * lax.rsqrt(variance + 1e-05) * gain[...]).astype(jnp.bfloat16)
    for copy in weights:
        copy.wait()


def attend(
    hidden_state,
    cross_query,
    source_keys,
    source_values,
    src_lengths,
    norm_gain,
    w_in,
    w_out,
):
    streams, width = hidden_state.shape
    span = source_keys.shape[1]
    arrays = (
        src_lengths,
        hidden_state,
        cross_query,
        source_keys,
        source_values,
        norm_gain.reshape(1, width),
        w_in,
        w_out,
    )
    vmem = pl.BlockSpec(memory_space=pltpu.VMEM)
    hbm = pl.BlockSpec(memory_space=pltpu.HBM)
    return pl.pallas_call(
        attend_kernel,
        out_shape=(
            pltpu.VMEM((streams, width), jnp.float32),
            pltpu.VMEM((streams, width), jnp.bfloat16),
            pltpu.VMEM(w_in.shape, w_in.dtype),
            pltpu.VMEM(w_out.shape, w_out.dtype),
        ),
        in_specs=[hbm] * 8,
        out_specs=(vmem,) * 4,
        scratch_shapes=[
            pltpu.SMEM((streams,), jnp.int32),
            pltpu.VMEM((streams, width), hidden_state.dtype),
            pltpu.VMEM((streams, width), cross_query.dtype),
            pltpu.VMEM((1, width), norm_gain.dtype),
            pltpu.VMEM((streams, span, width), source_keys.dtype),
            pltpu.VMEM((streams, span, width), source_values.dtype),
            pltpu.VMEM((streams * HEADS, span), jnp.float32),
            pltpu.SemaphoreType.DMA((6,)),
            pltpu.SemaphoreType.DMA((PIECES,)),
            pltpu.SemaphoreType.DMA((PIECES,)),
        ],
        compiler_params=pltpu.CompilerParams(vmem_limit_bytes=VMEM_LIMIT),
    )(*[pltpu.with_memory_space_constraint(array, pltpu.HBM) for array in arrays])


def feed_forward(rows, w_in, w_out, kind):
    def kernel(*refs):
        row_refs = refs[: len(rows)]
        w_in_ref, w_out_ref = refs[len(rows) : len(rows) + 2]
        stacked = jnp.concatenate([ref[...] for ref in row_refs], axis=0)
        units = jnp.dot(stacked, w_in_ref[...], preferred_element_type=jnp.float32)
        act = jnp.maximum(units, 0.0).astype(jnp.bfloat16)
        every = jnp.dot(act, w_out_ref[...], preferred_element_type=jnp.float32).astype(kind)
        start = 0
        for ref in refs[len(rows) + 2 :]:
            ref[...] = every[start : start + ref.shape[0]]
            start += ref.shape[0]

    vmem = pl.BlockSpec(memory_space=pltpu.VMEM)
    count = sum(part.shape[0] for part in rows)
    return pl.pallas_call(
        kernel,
        out_shape=[jax.ShapeDtypeStruct(part.shape, kind) for part in rows],
        in_specs=[vmem] * (len(rows) + 2),
        out_specs=[vmem] * len(rows),
        compiler_params=pltpu.CompilerParams(vmem_limit_bytes=VMEM_LIMIT),
        cost_estimate=pl.CostEstimate(
            flops=2 * count * w_in.size + 2 * count * w_out.size,
            transcendentals=0,
            bytes_accessed=2 * (w_in.size + w_out.size),
        ),
    )(*rows, w_in, w_out)


def step_on_device(
    hidden_state,
    cross_query,
    source_keys,
    source_values,
    src_lengths,
    norm_gain,
    w_in,
    w_out,
    expert_ids,
    route_weights,
):
    streams, width = hidden_state.shape
    devices = lax.axis_size("expert")
    experts_count = devices // SPLIT
    capacity = max(2, min(streams, 4 * streams * SPLIT // devices))
    direct = experts_count <= 4
    mixed, normed, w_in, w_out = attend(
        hidden_state,
        cross_query,
        source_keys,
        source_values,
        src_lengths,
        norm_gain,
        w_in,
        w_out,
    )
    group = lax.axis_index("expert") // SPLIT
    order = jnp.arange(experts_count, dtype=jnp.int32)
    if direct:
        order = order ^ group
    chosen = expert_ids[:, :, None] == order[None, None, :]
    weights = jnp.sum(jnp.where(chosen, route_weights[:, :, None], 0.0), axis=1)
    if capacity >= streams:
        blocks = [normed] * experts_count
    else:
        named = jnp.any(chosen, axis=1).astype(jnp.int32)
        rank = jnp.cumsum(named, axis=0) - named
        slots = jnp.arange(capacity, dtype=jnp.int32)
        placed = (named == 1)[None, :, :] & (rank[None, :, :] == slots[:, None, None])
        packed = jnp.einsum(
            "ctk,td->kcd",
            placed.astype(jnp.bfloat16),
            normed,
            preferred_element_type=jnp.float32,
        ).astype(jnp.bfloat16)
        blocks = [packed[index] for index in range(experts_count)]
    chips = SPLIT // CORES
    distances = far_first(experts_count)
    if direct:
        planes = {k: swap(blocks[k], k * SPLIT, devices) for k in distances}
        column = [blocks[0]] + [planes[k] for k in range(1, experts_count)]
    else:
        column = outer_exchange(blocks, devices)
    near = {0: jnp.concatenate(column, axis=0)}
    for step in range(1, chips):
        near[step] = swap(near[0], CORES * step, devices)
    far = {step: swap(near[step], 1, devices) for step in range(chips)}
    near_every = feed_forward([near[step] for step in range(chips)], w_in, w_out, jnp.float32)
    near_every, far = lax.optimization_barrier((near_every, far))
    far_sent = feed_forward([far[step] for step in range(chips)], w_in, w_out, jnp.bfloat16)
    pair = {}
    for step in range(chips):
        given = swap(far_sent[step], 1, devices)
        pair[step] = near_every[step] + given.astype(jnp.float32)
    total = pair[0]
    for step in range(1, chips):
        sent = pair[step].astype(jnp.bfloat16)
        total = total + swap(sent, CORES * step, devices).astype(jnp.float32)
    total = total.reshape(experts_count, capacity, width)
    result = mixed
    sent = total.astype(jnp.bfloat16)
    if direct:
        back = {k: swap(sent[k], k * SPLIT, devices) for k in distances}
        parts = [total[0]] + [back[k].astype(jnp.float32) for k in range(1, experts_count)]
    else:
        back = outer_exchange([sent[k] for k in range(experts_count)], devices)
        parts = [part.astype(jnp.float32) for part in back]
    for k, part in enumerate(parts):
        if capacity < streams:
            part = jnp.einsum(
                "ct,cd->td",
                placed[:, :, k].astype(jnp.float32),
                part,
                precision=lax.Precision.HIGHEST,
                preferred_element_type=jnp.float32,
            )
        result = result + weights[:, k : k + 1] * part
    return result.astype(jnp.bfloat16)


def solution(mesh):
    placed = (
        P(("group", "expert"), None),
        P(("group", "expert"), None),
        P(("group", "expert"), None, None),
        P(("group", "expert"), None, None),
        P(("group", "expert")),
        P(),
        P(None, "expert"),
        P("expert", None),
        P(("group", "expert"), None),
        P(("group", "expert"), None),
    )
    return jax.shard_map(
        step_on_device,
        mesh=mesh,
        in_specs=placed,
        out_specs=P(("group", "expert"), None),
        check_vma=False,
    )
```

```python
import jax
import jax.numpy as jnp
from jax import lax
from jax.experimental import pallas as pl
from jax.experimental.pallas import tpu as pltpu
from jax.sharding import PartitionSpec as P

HEADS = 16
SPLIT = 8
CORES = 2
PIECES = 4
VMEM_LIMIT = 16 * 1024 * 1024


def swap(value, distance, devices):
    pairs = [(source, source ^ distance) for source in range(devices)]
    return lax.ppermute(value, "expert", pairs)


def outer_exchange(blocks, devices):
    moved = lax.all_to_all(
        jnp.stack(blocks),
        "expert",
        split_axis=0,
        concat_axis=0,
        tiled=True,
        axis_index_groups=[list(range(inner, devices, SPLIT)) for inner in range(SPLIT)],
    )
    return [moved[index] for index in range(len(blocks))]


def far_first(count):
    return list(range(count - 1, 0, -1))


def attend_kernel(lengths_in, hidden_in, query_in, keys, values, gain_in, mixed, normed, lengths, hidden, query, gain, key_buf, value_buf, score_buf, small_sem, key_sem, value_sem):
    streams, width = hidden.shape
    span = key_buf.shape[1]
    head_size = width // HEADS
    group = key_buf.shape[0] // PIECES
    small = [
        pltpu.make_async_copy(query_in, query, small_sem.at[0]),
        pltpu.make_async_copy(lengths_in, lengths, small_sem.at[1]),
        pltpu.make_async_copy(hidden_in, hidden, small_sem.at[2]),
        pltpu.make_async_copy(gain_in, gain, small_sem.at[3]),
    ]
    pieces = [pl.ds(piece * group, group) for piece in range(PIECES)]
    key_copies = [pltpu.make_async_copy(keys.at[p], key_buf.at[p], key_sem.at[i]) for i, p in enumerate(pieces)]
    value_copies = [pltpu.make_async_copy(values.at[p], value_buf.at[p], value_sem.at[i]) for i, p in enumerate(pieces)]
    for copy in small + key_copies + value_copies:
        copy.start()
    owner = lax.broadcasted_iota(jnp.int32, (HEADS, width), 1) // head_size
    own = owner == lax.broadcasted_iota(jnp.int32, (HEADS, width), 0)
    position = lax.broadcasted_iota(jnp.int32, (HEADS, span), 1)
    small[0].wait()
    small[1].wait()
    for b in range(streams):
        if b % group == 0:
            key_copies[b // group].wait()
        spread = jnp.where(own, query[b : b + 1, :].astype(jnp.float32), 0.0).astype(jnp.bfloat16)
        scores = lax.dot_general(spread, key_buf[b], (((1,), (1,)), ((), ())), preferred_element_type=jnp.float32)
        scores = scores / jnp.sqrt(jnp.float32(head_size))
        score_buf[b * HEADS : (b + 1) * HEADS, :] = jnp.where(position < lengths[b], scores, -1e30)
    scores = score_buf[...]
    expo = jnp.exp(scores - jnp.max(scores, axis=-1, keepdims=True))
    score_buf[...] = expo / jnp.sum(expo, axis=-1, keepdims=True)
    for b in range(streams):
        if b % group == 0:
            value_copies[b // group].wait()
        probabilities = score_buf[b * HEADS : (b + 1) * HEADS, :].astype(jnp.bfloat16)
        every = jnp.dot(probabilities, value_buf[b], preferred_element_type=jnp.float32)
        for h in range(HEADS):
            lanes = slice(h * head_size, (h + 1) * head_size)
            mixed[b : b + 1, lanes] = every[h : h + 1, lanes]
    small[2].wait()
    small[3].wait()
    total = hidden[...].astype(jnp.float32) + mixed[...]
    mixed[...] = total
    centered = total - jnp.mean(total, axis=-1, keepdims=True)
    variance = jnp.mean(centered * centered, axis=-1, keepdims=True)
    normed[...] = (centered * lax.rsqrt(variance + 1e-05) * gain[...]).astype(jnp.bfloat16)


def attend(
    hidden_state,
    cross_query,
    source_keys,
    source_values,
    src_lengths,
    norm_gain,
):
    streams, width = hidden_state.shape
    span = source_keys.shape[1]
    arrays = (
        src_lengths,
        hidden_state,
        cross_query,
        source_keys,
        source_values,
        norm_gain.reshape(1, width),
    )
    vmem = pl.BlockSpec(memory_space=pltpu.VMEM)
    hbm = pl.BlockSpec(memory_space=pltpu.HBM)
    return pl.pallas_call(
        attend_kernel,
        out_shape=(
            pltpu.VMEM((streams, width), jnp.float32),
            pltpu.VMEM((streams, width), jnp.bfloat16),
        ),
        in_specs=[hbm] * 6,
        out_specs=(vmem, vmem),
        scratch_shapes=[
            pltpu.SMEM((streams,), jnp.int32),
            pltpu.VMEM((streams, width), hidden_state.dtype),
            pltpu.VMEM((streams, width), cross_query.dtype),
            pltpu.VMEM((1, width), norm_gain.dtype),
            pltpu.VMEM((streams, span, width), source_keys.dtype),
            pltpu.VMEM((streams, span, width), source_values.dtype),
            pltpu.VMEM((streams * HEADS, span), jnp.float32),
            pltpu.SemaphoreType.DMA((4,)),
            pltpu.SemaphoreType.DMA((PIECES,)),
            pltpu.SemaphoreType.DMA((PIECES,)),
        ],
        compiler_params=pltpu.CompilerParams(vmem_limit_bytes=VMEM_LIMIT),
    )(*[pltpu.with_memory_space_constraint(array, pltpu.HBM) for array in arrays])


def bring(array):
    def kernel(source, target, sem):
        copy = pltpu.make_async_copy(source, target, sem)
        copy.start()
        copy.wait()

    return pl.pallas_call(
        kernel,
        out_shape=pltpu.VMEM(array.shape, array.dtype),
        in_specs=[pl.BlockSpec(memory_space=pltpu.HBM)],
        out_specs=pl.BlockSpec(memory_space=pltpu.VMEM),
        scratch_shapes=[pltpu.SemaphoreType.DMA(())],
        compiler_params=pltpu.CompilerParams(vmem_limit_bytes=VMEM_LIMIT),
    )(pltpu.with_memory_space_constraint(array, pltpu.HBM))


def feed_forward(rows, w_in, w_out, kind):
    def kernel(*refs):
        row_refs = refs[: len(rows)]
        w_in_ref, w_out_ref = refs[len(rows) : len(rows) + 2]
        stacked = jnp.concatenate([ref[...] for ref in row_refs], axis=0)
        units = jnp.dot(stacked, w_in_ref[...], preferred_element_type=jnp.float32)
        act = jnp.maximum(units, 0.0).astype(jnp.bfloat16)
        every = jnp.dot(act, w_out_ref[...], preferred_element_type=jnp.float32).astype(kind)
        start = 0
        for ref in refs[len(rows) + 2 :]:
            ref[...] = every[start : start + ref.shape[0]]
            start += ref.shape[0]

    vmem = pl.BlockSpec(memory_space=pltpu.VMEM)
    count = sum(part.shape[0] for part in rows)
    return pl.pallas_call(
        kernel,
        out_shape=[jax.ShapeDtypeStruct(part.shape, kind) for part in rows],
        in_specs=[vmem] * (len(rows) + 2),
        out_specs=[vmem] * len(rows),
        compiler_params=pltpu.CompilerParams(vmem_limit_bytes=VMEM_LIMIT),
        cost_estimate=pl.CostEstimate(
            flops=2 * count * w_in.size + 2 * count * w_out.size,
            transcendentals=0,
            bytes_accessed=2 * (w_in.size + w_out.size),
        ),
    )(*rows, w_in, w_out)


def step_on_device(
    hidden_state,
    cross_query,
    source_keys,
    source_values,
    src_lengths,
    norm_gain,
    w_in,
    w_out,
    expert_ids,
    route_weights,
):
    streams, width = hidden_state.shape
    devices = lax.axis_size("expert")
    experts_count = devices // SPLIT
    capacity = max(2, min(streams, 4 * streams * SPLIT // devices))
    direct = experts_count <= 4
    mixed, normed = attend(
        hidden_state,
        cross_query,
        source_keys,
        source_values,
        src_lengths,
        norm_gain,
    )
    group = lax.axis_index("expert") // SPLIT
    order = jnp.arange(experts_count, dtype=jnp.int32)
    if direct:
        order = order ^ group
    chosen = expert_ids[:, :, None] == order[None, None, :]
    weights = jnp.sum(jnp.where(chosen, route_weights[:, :, None], 0.0), axis=1)
    if capacity >= streams:
        blocks = [normed] * experts_count
    else:
        named = jnp.any(chosen, axis=1).astype(jnp.int32)
        rank = jnp.cumsum(named, axis=0) - named
        slots = jnp.arange(capacity, dtype=jnp.int32)
        placed = (named == 1)[None, :, :] & (rank[None, :, :] == slots[:, None, None])
        packed = jnp.einsum(
            "ctk,td->kcd",
            placed.astype(jnp.bfloat16),
            normed,
            preferred_element_type=jnp.float32,
        ).astype(jnp.bfloat16)
        blocks = [packed[index] for index in range(experts_count)]
    chips = SPLIT // CORES
    distances = far_first(experts_count)
    if direct:
        planes = {k: swap(blocks[k], k * SPLIT, devices) for k in distances}
        column = [blocks[0]] + [planes[k] for k in range(1, experts_count)]
    else:
        column = outer_exchange(blocks, devices)
    near = {0: jnp.concatenate(column, axis=0)}
    for step in range(1, chips):
        near[step] = swap(near[0], CORES * step, devices)
    far = {step: swap(near[step], 1, devices) for step in range(chips)}
    w_in = bring(w_in)
    w_out = bring(w_out)
    near_every = feed_forward([near[step] for step in range(chips)], w_in, w_out, jnp.float32)
    near_every, far = lax.optimization_barrier((near_every, far))
    far_sent = feed_forward([far[step] for step in range(chips)], w_in, w_out, jnp.bfloat16)
    pair = {}
    for step in range(chips):
        given = swap(far_sent[step], 1, devices)
        pair[step] = near_every[step] + given.astype(jnp.float32)
    total = pair[0]
    for step in range(1, chips):
        sent = pair[step].astype(jnp.bfloat16)
        total = total + swap(sent, CORES * step, devices).astype(jnp.float32)
    total = total.reshape(experts_count, capacity, width)
    result = mixed
    sent = total.astype(jnp.bfloat16)
    if direct:
        back = {k: swap(sent[k], k * SPLIT, devices) for k in distances}
        parts = [total[0]] + [back[k].astype(jnp.float32) for k in range(1, experts_count)]
    else:
        back = outer_exchange([sent[k] for k in range(experts_count)], devices)
        parts = [part.astype(jnp.float32) for part in back]
    for k, part in enumerate(parts):
        if capacity < streams:
            part = jnp.einsum(
                "ct,cd->td",
                placed[:, :, k].astype(jnp.float32),
                part,
                precision=lax.Precision.HIGHEST,
                preferred_element_type=jnp.float32,
            )
        result = result + weights[:, k : k + 1] * part
    return result.astype(jnp.bfloat16)


def solution(mesh):
    placed = (
        P(("group", "expert"), None),
        P(("group", "expert"), None),
        P(("group", "expert"), None, None),
        P(("group", "expert"), None, None),
        P(("group", "expert")),
        P(),
        P(None, "expert"),
        P("expert", None),
        P(("group", "expert"), None),
        P(("group", "expert"), None),
    )
    return jax.shard_map(
        step_on_device,
        mesh=mesh,
        in_specs=placed,
        out_specs=P(("group", "expert"), None),
        check_vma=False,
    )
```

```python
import jax
import jax.numpy as jnp
from jax import lax
from jax.experimental import pallas as pl
from jax.experimental.pallas import tpu as pltpu
from jax.sharding import PartitionSpec as P

HEADS = 16
SPLIT = 8
CORES = 2
PIECES = 4
VMEM_LIMIT = 16 * 1024 * 1024


def swap(value, distance, devices):
    pairs = [(source, source ^ distance) for source in range(devices)]
    return lax.ppermute(value, "expert", pairs)


def outer_exchange(blocks, devices):
    moved = lax.all_to_all(
        jnp.stack(blocks),
        "expert",
        split_axis=0,
        concat_axis=0,
        tiled=True,
        axis_index_groups=[list(range(inner, devices, SPLIT)) for inner in range(SPLIT)],
    )
    return [moved[index] for index in range(len(blocks))]


def far_first(count):
    return list(range(count - 1, 0, -1))


def attend_kernel(lengths_in, hidden_in, query_in, keys, values, gain_in, mixed, normed, lengths, hidden, query, gain, key_buf, value_buf, score_buf, small_sem, key_sem, value_sem):
    streams, width = hidden.shape
    span = key_buf.shape[1]
    head_size = width // HEADS
    group = key_buf.shape[0] // PIECES
    small = [
        pltpu.make_async_copy(query_in, query, small_sem.at[0]),
        pltpu.make_async_copy(lengths_in, lengths, small_sem.at[1]),
        pltpu.make_async_copy(hidden_in, hidden, small_sem.at[2]),
        pltpu.make_async_copy(gain_in, gain, small_sem.at[3]),
    ]
    pieces = [pl.ds(piece * group, group) for piece in range(PIECES)]
    key_copies = [pltpu.make_async_copy(keys.at[p], key_buf.at[p], key_sem.at[i]) for i, p in enumerate(pieces)]
    value_copies = [pltpu.make_async_copy(values.at[p], value_buf.at[p], value_sem.at[i]) for i, p in enumerate(pieces)]
    for copy in small + key_copies + value_copies:
        copy.start()
    owner = lax.broadcasted_iota(jnp.int32, (HEADS, width), 1) // head_size
    own = owner == lax.broadcasted_iota(jnp.int32, (HEADS, width), 0)
    position = lax.broadcasted_iota(jnp.int32, (HEADS, span), 1)
    small[0].wait()
    small[1].wait()
    for b in range(streams):
        if b % group == 0:
            key_copies[b // group].wait()
        spread = jnp.where(own, query[b : b + 1, :].astype(jnp.float32), 0.0).astype(jnp.bfloat16)
        scores = lax.dot_general(spread, key_buf[b], (((1,), (1,)), ((), ())), preferred_element_type=jnp.float32)
        scores = scores / jnp.sqrt(jnp.float32(head_size))
        score_buf[b * HEADS : (b + 1) * HEADS, :] = jnp.where(position < lengths[b], scores, -1e30)
    scores = score_buf[...]
    expo = jnp.exp(scores - jnp.max(scores, axis=-1, keepdims=True))
    score_buf[...] = expo / jnp.sum(expo, axis=-1, keepdims=True)
    for b in range(streams):
        if b % group == 0:
            value_copies[b // group].wait()
        probabilities = score_buf[b * HEADS : (b + 1) * HEADS, :].astype(jnp.bfloat16)
        every = jnp.dot(probabilities, value_buf[b], preferred_element_type=jnp.float32)
        for h in range(HEADS):
            lanes = slice(h * head_size, (h + 1) * head_size)
            mixed[b : b + 1, lanes] = every[h : h + 1, lanes]
    small[2].wait()
    small[3].wait()
    total = hidden[...].astype(jnp.float32) + mixed[...]
    mixed[...] = total
    centered = total - jnp.mean(total, axis=-1, keepdims=True)
    variance = jnp.mean(centered * centered, axis=-1, keepdims=True)
    normed[...] = (centered * lax.rsqrt(variance + 1e-05) * gain[...]).astype(jnp.bfloat16)


def attend(
    hidden_state,
    cross_query,
    source_keys,
    source_values,
    src_lengths,
    norm_gain,
):
    streams, width = hidden_state.shape
    span = source_keys.shape[1]
    arrays = (
        src_lengths,
        hidden_state,
        cross_query,
        source_keys,
        source_values,
        norm_gain.reshape(1, width),
    )
    vmem = pl.BlockSpec(memory_space=pltpu.VMEM)
    hbm = pl.BlockSpec(memory_space=pltpu.HBM)
    return pl.pallas_call(
        attend_kernel,
        out_shape=(
            pltpu.VMEM((streams, width), jnp.float32),
            pltpu.VMEM((streams, width), jnp.bfloat16),
        ),
        in_specs=[hbm] * 6,
        out_specs=(vmem, vmem),
        scratch_shapes=[
            pltpu.SMEM((streams,), jnp.int32),
            pltpu.VMEM((streams, width), hidden_state.dtype),
            pltpu.VMEM((streams, width), cross_query.dtype),
            pltpu.VMEM((1, width), norm_gain.dtype),
            pltpu.VMEM((streams, span, width), source_keys.dtype),
            pltpu.VMEM((streams, span, width), source_values.dtype),
            pltpu.VMEM((streams * HEADS, span), jnp.float32),
            pltpu.SemaphoreType.DMA((4,)),
            pltpu.SemaphoreType.DMA((PIECES,)),
            pltpu.SemaphoreType.DMA((PIECES,)),
        ],
        compiler_params=pltpu.CompilerParams(vmem_limit_bytes=VMEM_LIMIT),
    )(*[pltpu.with_memory_space_constraint(array, pltpu.HBM) for array in arrays])


def bring(array):
    def kernel(source, target, sem):
        copy = pltpu.make_async_copy(source, target, sem)
        copy.start()
        copy.wait()

    return pl.pallas_call(
        kernel,
        out_shape=pltpu.VMEM(array.shape, array.dtype),
        in_specs=[pl.BlockSpec(memory_space=pltpu.HBM)],
        out_specs=pl.BlockSpec(memory_space=pltpu.VMEM),
        scratch_shapes=[pltpu.SemaphoreType.DMA(())],
        compiler_params=pltpu.CompilerParams(vmem_limit_bytes=VMEM_LIMIT),
    )(pltpu.with_memory_space_constraint(array, pltpu.HBM))


def feed_forward(rows, w_in, w_out, kind):
    def kernel(*refs):
        row_refs = refs[: len(rows)]
        w_in_ref, w_out_ref = refs[len(rows) : len(rows) + 2]
        stacked = jnp.concatenate([ref[...] for ref in row_refs], axis=0)
        units = jnp.dot(stacked, w_in_ref[...], preferred_element_type=jnp.float32)
        act = jnp.maximum(units, 0.0).astype(jnp.bfloat16)
        every = jnp.dot(act, w_out_ref[...], preferred_element_type=jnp.float32).astype(kind)
        start = 0
        for ref in refs[len(rows) + 2 :]:
            ref[...] = every[start : start + ref.shape[0]]
            start += ref.shape[0]

    vmem = pl.BlockSpec(memory_space=pltpu.VMEM)
    count = sum(part.shape[0] for part in rows)
    return pl.pallas_call(
        kernel,
        out_shape=[jax.ShapeDtypeStruct(part.shape, kind) for part in rows],
        in_specs=[vmem] * (len(rows) + 2),
        out_specs=[vmem] * len(rows),
        compiler_params=pltpu.CompilerParams(vmem_limit_bytes=VMEM_LIMIT),
        cost_estimate=pl.CostEstimate(
            flops=2 * count * w_in.size + 2 * count * w_out.size,
            transcendentals=0,
            bytes_accessed=2 * (w_in.size + w_out.size),
        ),
    )(*rows, w_in, w_out)


def step_on_device(
    hidden_state,
    cross_query,
    source_keys,
    source_values,
    src_lengths,
    norm_gain,
    w_in,
    w_out,
    expert_ids,
    route_weights,
):
    streams, width = hidden_state.shape
    devices = lax.axis_size("expert")
    experts_count = devices // SPLIT
    capacity = max(2, min(streams, 4 * streams * SPLIT // devices))
    direct = experts_count <= 4
    group = lax.shift_right_logical(lax.axis_index("expert"), SPLIT.bit_length() - 1)
    group, src_lengths = lax.optimization_barrier((group, src_lengths))
    mixed, normed = attend(
        hidden_state,
        cross_query,
        source_keys,
        source_values,
        src_lengths,
        norm_gain,
    )
    order = jnp.arange(experts_count, dtype=jnp.int32)
    if direct:
        order = order ^ group
    chosen = expert_ids[:, :, None] == order[None, None, :]
    weights = jnp.sum(jnp.where(chosen, route_weights[:, :, None], 0.0), axis=1)
    if capacity >= streams:
        blocks = [normed] * experts_count
    else:
        named = jnp.any(chosen, axis=1).astype(jnp.int32)
        rank = jnp.cumsum(named, axis=0) - named
        slots = jnp.arange(capacity, dtype=jnp.int32)
        placed = (named == 1)[None, :, :] & (rank[None, :, :] == slots[:, None, None])
        packed = jnp.einsum(
            "ctk,td->kcd",
            placed.astype(jnp.bfloat16),
            normed,
            preferred_element_type=jnp.float32,
        ).astype(jnp.bfloat16)
        blocks = [packed[index] for index in range(experts_count)]
    chips = SPLIT // CORES
    distances = far_first(experts_count)
    if direct:
        planes = {k: swap(blocks[k], k * SPLIT, devices) for k in distances}
        column = [blocks[0]] + [planes[k] for k in range(1, experts_count)]
    else:
        column = outer_exchange(blocks, devices)
    near = {0: jnp.concatenate(column, axis=0)}
    for step in range(1, chips):
        near[step] = swap(near[0], CORES * step, devices)
    far = {step: swap(near[step], 1, devices) for step in range(chips)}
    w_in = bring(w_in)
    w_out = bring(w_out)
    near_every = feed_forward([near[step] for step in range(chips)], w_in, w_out, jnp.float32)
    near_every, far = lax.optimization_barrier((near_every, far))
    far_sent = feed_forward([far[step] for step in range(chips)], w_in, w_out, jnp.bfloat16)
    pair = [None] * chips
    for step in range(chips):
        pair[step] = (near_every[step], swap(far_sent[step], 1, devices))
    bounds = [("reduce_chip", slice(capacity, None)), ("reduce_own", slice(0, capacity))]
    if not direct:
        bounds = [("reduce_chip", slice(None))]
    sums = {}
    for name, place in bounds:
        joined = [mine[place] + other[place].astype(jnp.float32) for mine, other in pair]
        sums[name] = joined[0]
        for step in range(1, chips):
            given = swap(joined[step].astype(jnp.bfloat16), CORES * step, devices)
            sums[name] = sums[name] + given.astype(jnp.float32)
    total = sums["reduce_chip"].reshape(-1, capacity, width)
    result = mixed
    sent = total.astype(jnp.bfloat16)
    if direct:
        back = {k: swap(sent[k - 1], k * SPLIT, devices) for k in distances}
        parts = [sums["reduce_own"]]
        parts += [back[k].astype(jnp.float32) for k in range(1, experts_count)]
    else:
        back = outer_exchange([sent[k] for k in range(experts_count)], devices)
        parts = [part.astype(jnp.float32) for part in back]
    for k, part in enumerate(parts):
        if capacity < streams:
            part = jnp.einsum(
                "ct,cd->td",
                placed[:, :, k].astype(jnp.float32),
                part,
                precision=lax.Precision.HIGHEST,
                preferred_element_type=jnp.float32,
            )
        result = result + weights[:, k : k + 1] * part
    return result.astype(jnp.bfloat16)


def solution(mesh):
    placed = (
        P(("group", "expert"), None),
        P(("group", "expert"), None),
        P(("group", "expert"), None, None),
        P(("group", "expert"), None, None),
        P(("group", "expert")),
        P(),
        P(None, "expert"),
        P("expert", None),
        P(("group", "expert"), None),
        P(("group", "expert"), None),
    )
    return jax.shard_map(
        step_on_device,
        mesh=mesh,
        in_specs=placed,
        out_specs=P(("group", "expert"), None),
        check_vma=False,
    )
```

```python
import jax
import jax.numpy as jnp
from jax import lax
from jax.experimental import pallas as pl
from jax.experimental.pallas import tpu as pltpu
from jax.sharding import PartitionSpec as P

HEADS = 16
SPLIT = 8
CORES = 2
PIECES = 4
VMEM_LIMIT = 16 * 1024 * 1024


def swap(value, distance, devices):
    pairs = [(source, source ^ distance) for source in range(devices)]
    return lax.ppermute(value, "expert", pairs)


def outer_exchange(blocks, devices):
    moved = lax.all_to_all(
        jnp.stack(blocks),
        "expert",
        split_axis=0,
        concat_axis=0,
        tiled=True,
        axis_index_groups=[list(range(inner, devices, SPLIT)) for inner in range(SPLIT)],
    )
    return [moved[index] for index in range(len(blocks))]


def far_first(count):
    return list(range(count - 1, 0, -1))


def attend_kernel(lengths_in, hidden_in, query_in, keys, values, gain_in, w_in_from, mixed, normed, w_in, lengths, hidden, query, gain, key_buf, value_buf, score_buf, small_sem, key_sem, value_sem):
    streams, width = hidden.shape
    span = key_buf.shape[1]
    head_size = width // HEADS
    group = key_buf.shape[0] // PIECES
    small = [
        pltpu.make_async_copy(query_in, query, small_sem.at[0]),
        pltpu.make_async_copy(lengths_in, lengths, small_sem.at[1]),
        pltpu.make_async_copy(hidden_in, hidden, small_sem.at[2]),
        pltpu.make_async_copy(gain_in, gain, small_sem.at[3]),
    ]
    pieces = [pl.ds(piece * group, group) for piece in range(PIECES)]
    key_copies = [pltpu.make_async_copy(keys.at[p], key_buf.at[p], key_sem.at[i]) for i, p in enumerate(pieces)]
    value_copies = [pltpu.make_async_copy(values.at[p], value_buf.at[p], value_sem.at[i]) for i, p in enumerate(pieces)]
    weight_copy = pltpu.make_async_copy(w_in_from, w_in, small_sem.at[4])
    for copy in small + key_copies + value_copies + [weight_copy]:
        copy.start()
    owner = lax.broadcasted_iota(jnp.int32, (HEADS, width), 1) // head_size
    own = owner == lax.broadcasted_iota(jnp.int32, (HEADS, width), 0)
    position = lax.broadcasted_iota(jnp.int32, (HEADS, span), 1)
    small[0].wait()
    small[1].wait()
    for b in range(streams):
        if b % group == 0:
            key_copies[b // group].wait()
        spread = jnp.where(own, query[b : b + 1, :].astype(jnp.float32), 0.0).astype(jnp.bfloat16)
        scores = lax.dot_general(spread, key_buf[b], (((1,), (1,)), ((), ())), preferred_element_type=jnp.float32)
        scores = scores / jnp.sqrt(jnp.float32(head_size))
        score_buf[b * HEADS : (b + 1) * HEADS, :] = jnp.where(position < lengths[b], scores, -1e30)
    scores = score_buf[...]
    expo = jnp.exp(scores - jnp.max(scores, axis=-1, keepdims=True))
    score_buf[...] = expo / jnp.sum(expo, axis=-1, keepdims=True)
    for b in range(streams):
        if b % group == 0:
            value_copies[b // group].wait()
        probabilities = score_buf[b * HEADS : (b + 1) * HEADS, :].astype(jnp.bfloat16)
        every = jnp.dot(probabilities, value_buf[b], preferred_element_type=jnp.float32)
        for h in range(HEADS):
            lanes = slice(h * head_size, (h + 1) * head_size)
            mixed[b : b + 1, lanes] = every[h : h + 1, lanes]
    small[2].wait()
    small[3].wait()
    total = hidden[...].astype(jnp.float32) + mixed[...]
    mixed[...] = total
    centered = total - jnp.mean(total, axis=-1, keepdims=True)
    variance = jnp.mean(centered * centered, axis=-1, keepdims=True)
    normed[...] = (centered * lax.rsqrt(variance + 1e-05) * gain[...]).astype(jnp.bfloat16)
    weight_copy.wait()


def attend(
    hidden_state,
    cross_query,
    source_keys,
    source_values,
    src_lengths,
    norm_gain,
    w_in,
):
    streams, width = hidden_state.shape
    span = source_keys.shape[1]
    arrays = (
        src_lengths,
        hidden_state,
        cross_query,
        source_keys,
        source_values,
        norm_gain.reshape(1, width),
        w_in,
    )
    vmem = pl.BlockSpec(memory_space=pltpu.VMEM)
    hbm = pl.BlockSpec(memory_space=pltpu.HBM)
    return pl.pallas_call(
        attend_kernel,
        out_shape=(
            pltpu.VMEM((streams, width), jnp.float32),
            pltpu.VMEM((streams, width), jnp.bfloat16),
            pltpu.VMEM(w_in.shape, w_in.dtype),
        ),
        in_specs=[hbm] * 7,
        out_specs=(vmem,) * 3,
        scratch_shapes=[
            pltpu.SMEM((streams,), jnp.int32),
            pltpu.VMEM((streams, width), hidden_state.dtype),
            pltpu.VMEM((streams, width), cross_query.dtype),
            pltpu.VMEM((1, width), norm_gain.dtype),
            pltpu.VMEM((streams, span, width), source_keys.dtype),
            pltpu.VMEM((streams, span, width), source_values.dtype),
            pltpu.VMEM((streams * HEADS, span), jnp.float32),
            pltpu.SemaphoreType.DMA((5,)),
            pltpu.SemaphoreType.DMA((PIECES,)),
            pltpu.SemaphoreType.DMA((PIECES,)),
        ],
        compiler_params=pltpu.CompilerParams(vmem_limit_bytes=VMEM_LIMIT),
    )(*[pltpu.with_memory_space_constraint(array, pltpu.HBM) for array in arrays])


def bring(array):
    def kernel(source, target, sem):
        copy = pltpu.make_async_copy(source, target, sem)
        copy.start()
        copy.wait()

    return pl.pallas_call(
        kernel,
        out_shape=pltpu.VMEM(array.shape, array.dtype),
        in_specs=[pl.BlockSpec(memory_space=pltpu.HBM)],
        out_specs=pl.BlockSpec(memory_space=pltpu.VMEM),
        scratch_shapes=[pltpu.SemaphoreType.DMA(())],
        compiler_params=pltpu.CompilerParams(vmem_limit_bytes=VMEM_LIMIT),
    )(pltpu.with_memory_space_constraint(array, pltpu.HBM))


def feed_forward(rows, weights, cuts):
    kinds = [jnp.float32] + [jnp.bfloat16] * (len(rows) - 1)
    height, width = rows[0].shape
    parts = [(block, start, end) for block in range(len(rows)) for start, end in cuts]

    def kernel(*refs):
        row_refs = refs[: len(rows)]
        weight_refs = refs[len(rows) : len(rows) + 2 * len(weights)]
        out_refs = refs[len(rows) + 2 * len(weights) :]
        stacked = jnp.concatenate([ref[...] for ref in row_refs], axis=0)
        every = None
        for w_in_ref, w_out_ref in zip(weight_refs[::2], weight_refs[1::2]):
            units = jnp.dot(stacked, w_in_ref[...], preferred_element_type=jnp.float32)
            act = jnp.maximum(units, 0.0).astype(jnp.bfloat16)
            some = jnp.dot(act, w_out_ref[...], preferred_element_type=jnp.float32)
            every = some if every is None else every + some
        for ref, (block, start, end) in zip(out_refs, parts):
            ref[...] = every[block * height + start : block * height + end].astype(kinds[block])

    vmem = pl.BlockSpec(memory_space=pltpu.VMEM)
    flat = [array for pair in weights for array in pair]
    size = sum(array.size for array in flat)
    out = pl.pallas_call(
        kernel,
        out_shape=[
            jax.ShapeDtypeStruct((end - start, width), kinds[block]) for block, start, end in parts
        ],
        in_specs=[vmem] * (len(rows) + len(flat)),
        out_specs=[vmem] * len(parts),
        compiler_params=pltpu.CompilerParams(vmem_limit_bytes=VMEM_LIMIT),
        cost_estimate=pl.CostEstimate(
            flops=2 * len(rows) * height * size, transcendentals=0, bytes_accessed=2 * size
        ),
    )(*rows, *flat)
    return [out[block * len(cuts) : (block + 1) * len(cuts)] for block in range(len(rows))]


def step_on_device(
    hidden_state,
    cross_query,
    source_keys,
    source_values,
    src_lengths,
    norm_gain,
    w_in,
    w_out,
    expert_ids,
    route_weights,
):
    streams, width = hidden_state.shape
    devices = lax.axis_size("expert")
    experts_count = devices // SPLIT
    capacity = max(2, min(streams, 4 * streams * SPLIT // devices))
    direct = experts_count <= 4
    group = lax.shift_right_logical(lax.axis_index("expert"), SPLIT.bit_length() - 1)
    group, src_lengths = lax.optimization_barrier((group, src_lengths))
    mixed, normed, w_in = attend(
        hidden_state,
        cross_query,
        source_keys,
        source_values,
        src_lengths,
        norm_gain,
        w_in,
    )
    order = jnp.arange(experts_count, dtype=jnp.int32)
    if direct:
        order = order ^ group
    chosen = expert_ids[:, :, None] == order[None, None, :]
    weights = jnp.sum(jnp.where(chosen, route_weights[:, :, None], 0.0), axis=1)
    if capacity >= streams:
        blocks = [normed] * experts_count
    else:
        named = jnp.any(chosen, axis=1).astype(jnp.int32)
        rank = jnp.cumsum(named, axis=0) - named
        slots = jnp.arange(capacity, dtype=jnp.int32)
        placed = (named == 1)[None, :, :] & (rank[None, :, :] == slots[:, None, None])
        packed = jnp.einsum(
            "ctk,td->kcd",
            placed.astype(jnp.bfloat16),
            normed,
            preferred_element_type=jnp.float32,
        ).astype(jnp.bfloat16)
        blocks = [packed[index] for index in range(experts_count)]
    chips = SPLIT // CORES
    distances = far_first(experts_count)
    if direct:
        planes = {k: swap(blocks[k], k * SPLIT, devices) for k in distances}
        column = [blocks[0]] + [planes[k] for k in range(1, experts_count)]
    else:
        column = outer_exchange(blocks, devices)
    near = {0: jnp.concatenate(column, axis=0)}
    for step in range(1, chips):
        near[step] = swap(near[0], CORES * step, devices)
    other_in = swap(w_in, 1, devices)
    w_out = bring(w_out)
    other_out = swap(w_out, 1, devices)
    height = near[0].shape[0]
    cuts = [("reduce_chip", 0, height)]
    if direct:
        cuts = [("reduce_chip", capacity, height), ("reduce_own", 0, capacity)]
    parts = feed_forward(
        [near[step] for step in range(chips)],
        [(w_in, w_out), (other_in, other_out)],
        [(start, end) for _, start, end in cuts],
    )
    sums = {}
    for place, (name, _, _) in enumerate(cuts):
        sums[name] = parts[0][place]
        for step in range(1, chips):
            given = swap(parts[step][place], CORES * step, devices)
            sums[name] = sums[name] + given.astype(jnp.float32)
    total = sums["reduce_chip"].reshape(-1, capacity, width)
    result = mixed
    sent = total.astype(jnp.bfloat16)
    if direct:
        back = {k: swap(sent[k - 1], k * SPLIT, devices) for k in distances}
        parts = [sums["reduce_own"]]
        parts += [back[k].astype(jnp.float32) for k in range(1, experts_count)]
    else:
        back = outer_exchange([sent[k] for k in range(experts_count)], devices)
        parts = [part.astype(jnp.float32) for part in back]
    for k, part in enumerate(parts):
        if capacity < streams:
            part = jnp.einsum(
                "ct,cd->td",
                placed[:, :, k].astype(jnp.float32),
                part,
                precision=lax.Precision.HIGHEST,
                preferred_element_type=jnp.float32,
            )
        result = result + weights[:, k : k + 1] * part
    return result.astype(jnp.bfloat16)


def solution(mesh):
    placed = (
        P(("group", "expert"), None),
        P(("group", "expert"), None),
        P(("group", "expert"), None, None),
        P(("group", "expert"), None, None),
        P(("group", "expert")),
        P(),
        P(None, "expert"),
        P("expert", None),
        P(("group", "expert"), None),
        P(("group", "expert"), None),
    )
    return jax.shard_map(
        step_on_device,
        mesh=mesh,
        in_specs=placed,
        out_specs=P(("group", "expert"), None),
        check_vma=False,
    )
```

```python
import jax
import jax.numpy as jnp
from jax import lax
from jax.experimental import pallas as pl
from jax.experimental.pallas import tpu as pltpu
from jax.sharding import PartitionSpec as P

HEADS = 16
SPLIT = 8
CORES = 2
PIECES = 4
VMEM_LIMIT = 16 * 1024 * 1024


def swap(value, distance, devices):
    pairs = [(source, source ^ distance) for source in range(devices)]
    return lax.ppermute(value, "expert", pairs)


def outer_exchange(blocks, devices):
    moved = lax.all_to_all(
        jnp.stack(blocks),
        "expert",
        split_axis=0,
        concat_axis=0,
        tiled=True,
        axis_index_groups=[list(range(inner, devices, SPLIT)) for inner in range(SPLIT)],
    )
    return [moved[index] for index in range(len(blocks))]


def far_first(count):
    return list(range(count - 1, 0, -1))


def attend_kernel(lengths_in, hidden_in, query_in, keys, values, gain_in, w_in_from, mixed, normed, w_in, lengths, hidden, query, gain, key_buf, value_buf, score_buf, small_sem, key_sem, value_sem):
    streams, width = hidden.shape
    span = key_buf.shape[1]
    head_size = width // HEADS
    group = key_buf.shape[0] // PIECES
    small = [
        pltpu.make_async_copy(query_in, query, small_sem.at[0]),
        pltpu.make_async_copy(lengths_in, lengths, small_sem.at[1]),
        pltpu.make_async_copy(hidden_in, hidden, small_sem.at[2]),
        pltpu.make_async_copy(gain_in, gain, small_sem.at[3]),
    ]
    pieces = [pl.ds(piece * group, group) for piece in range(PIECES)]
    key_copies = [pltpu.make_async_copy(keys.at[p], key_buf.at[p], key_sem.at[i]) for i, p in enumerate(pieces)]
    value_copies = [pltpu.make_async_copy(values.at[p], value_buf.at[p], value_sem.at[i]) for i, p in enumerate(pieces)]
    weight_copy = pltpu.make_async_copy(w_in_from, w_in, small_sem.at[4])
    for copy in small + key_copies + value_copies + [weight_copy]:
        copy.start()
    owner = lax.broadcasted_iota(jnp.int32, (HEADS, width), 1) // head_size
    own = owner == lax.broadcasted_iota(jnp.int32, (HEADS, width), 0)
    position = lax.broadcasted_iota(jnp.int32, (HEADS, span), 1)
    small[0].wait()
    small[1].wait()
    for b in range(streams):
        if b % group == 0:
            key_copies[b // group].wait()
        spread = jnp.where(own, query[b : b + 1, :].astype(jnp.float32), 0.0).astype(jnp.bfloat16)
        scores = lax.dot_general(spread, key_buf[b], (((1,), (1,)), ((), ())), preferred_element_type=jnp.float32)
        scores = scores / jnp.sqrt(jnp.float32(head_size))
        score_buf[b * HEADS : (b + 1) * HEADS, :] = jnp.where(position < lengths[b], scores, -1e30)
    scores = score_buf[...]
    expo = jnp.exp(scores - jnp.max(scores, axis=-1, keepdims=True))
    score_buf[...] = expo / jnp.sum(expo, axis=-1, keepdims=True)
    for b in range(streams):
        if b % group == 0:
            value_copies[b // group].wait()
        probabilities = score_buf[b * HEADS : (b + 1) * HEADS, :].astype(jnp.bfloat16)
        every = jnp.dot(probabilities, value_buf[b], preferred_element_type=jnp.float32)
        for h in range(HEADS):
            lanes = slice(h * head_size, (h + 1) * head_size)
            mixed[b : b + 1, lanes] = every[h : h + 1, lanes]
    small[2].wait()
    small[3].wait()
    total = hidden[...].astype(jnp.float32) + mixed[...]
    mixed[...] = total
    centered = total - jnp.mean(total, axis=-1, keepdims=True)
    variance = jnp.mean(centered * centered, axis=-1, keepdims=True)
    normed[...] = (centered * lax.rsqrt(variance + 1e-05) * gain[...]).astype(jnp.bfloat16)
    weight_copy.wait()


def attend(
    hidden_state,
    cross_query,
    source_keys,
    source_values,
    src_lengths,
    norm_gain,
    w_in,
):
    streams, width = hidden_state.shape
    span = source_keys.shape[1]
    arrays = (
        src_lengths,
        hidden_state,
        cross_query,
        source_keys,
        source_values,
        norm_gain.reshape(1, width),
        w_in,
    )
    vmem = pl.BlockSpec(memory_space=pltpu.VMEM)
    hbm = pl.BlockSpec(memory_space=pltpu.HBM)
    return pl.pallas_call(
        attend_kernel,
        out_shape=(
            pltpu.VMEM((streams, width), jnp.float32),
            pltpu.VMEM((streams, width), jnp.bfloat16),
            pltpu.VMEM(w_in.shape, w_in.dtype),
        ),
        in_specs=[hbm] * 7,
        out_specs=(vmem,) * 3,
        scratch_shapes=[
            pltpu.SMEM((streams,), jnp.int32),
            pltpu.VMEM((streams, width), hidden_state.dtype),
            pltpu.VMEM((streams, width), cross_query.dtype),
            pltpu.VMEM((1, width), norm_gain.dtype),
            pltpu.VMEM((streams, span, width), source_keys.dtype),
            pltpu.VMEM((streams, span, width), source_values.dtype),
            pltpu.VMEM((streams * HEADS, span), jnp.float32),
            pltpu.SemaphoreType.DMA((5,)),
            pltpu.SemaphoreType.DMA((PIECES,)),
            pltpu.SemaphoreType.DMA((PIECES,)),
        ],
        compiler_params=pltpu.CompilerParams(vmem_limit_bytes=VMEM_LIMIT),
    )(*[pltpu.with_memory_space_constraint(array, pltpu.HBM) for array in arrays])


def bring(array):
    def kernel(source, target, sem):
        copy = pltpu.make_async_copy(source, target, sem)
        copy.start()
        copy.wait()

    return pl.pallas_call(
        kernel,
        out_shape=pltpu.VMEM(array.shape, array.dtype),
        in_specs=[pl.BlockSpec(memory_space=pltpu.HBM)],
        out_specs=pl.BlockSpec(memory_space=pltpu.VMEM),
        scratch_shapes=[pltpu.SemaphoreType.DMA(())],
        compiler_params=pltpu.CompilerParams(vmem_limit_bytes=VMEM_LIMIT),
    )(pltpu.with_memory_space_constraint(array, pltpu.HBM))


def feed_forward(rows, weights):
    kinds = [jnp.float32] + [jnp.bfloat16] * (len(rows) - 1)
    height, width = rows[0].shape

    def kernel(*refs):
        row_refs = refs[: len(rows)]
        weight_refs = refs[len(rows) : len(rows) + 2 * len(weights)]
        out_refs = refs[len(rows) + 2 * len(weights) :]
        stacked = jnp.concatenate([ref[...] for ref in row_refs], axis=0)
        every = None
        for w_in_ref, w_out_ref in zip(weight_refs[::2], weight_refs[1::2]):
            units = jnp.dot(stacked, w_in_ref[...], preferred_element_type=jnp.float32)
            act = jnp.maximum(units, 0.0).astype(jnp.bfloat16)
            some = jnp.dot(act, w_out_ref[...], preferred_element_type=jnp.float32)
            every = some if every is None else every + some
        for block, ref in enumerate(out_refs):
            ref[...] = every[block * height : (block + 1) * height].astype(kinds[block])

    vmem = pl.BlockSpec(memory_space=pltpu.VMEM)
    flat = [array for pair in weights for array in pair]
    size = sum(array.size for array in flat)
    return pl.pallas_call(
        kernel,
        out_shape=[jax.ShapeDtypeStruct((height, width), kind) for kind in kinds],
        in_specs=[vmem] * (len(rows) + len(flat)),
        out_specs=[vmem] * len(rows),
        compiler_params=pltpu.CompilerParams(vmem_limit_bytes=VMEM_LIMIT),
        cost_estimate=pl.CostEstimate(
            flops=2 * len(rows) * height * size, transcendentals=0, bytes_accessed=2 * size
        ),
    )(*rows, *flat)


def step_on_device(
    hidden_state,
    cross_query,
    source_keys,
    source_values,
    src_lengths,
    norm_gain,
    w_in,
    w_out,
    expert_ids,
    route_weights,
):
    streams, width = hidden_state.shape
    devices = lax.axis_size("expert")
    experts_count = devices // SPLIT
    capacity = max(2, min(streams, 4 * streams * SPLIT // devices))
    direct = experts_count <= 4
    group = lax.shift_right_logical(lax.axis_index("expert"), SPLIT.bit_length() - 1)
    group, src_lengths = lax.optimization_barrier((group, src_lengths))
    mixed, normed, w_in = attend(
        hidden_state,
        cross_query,
        source_keys,
        source_values,
        src_lengths,
        norm_gain,
        w_in,
    )
    order = jnp.arange(experts_count, dtype=jnp.int32)
    if direct:
        order = order ^ group
    chosen = expert_ids[:, :, None] == order[None, None, :]
    weights = jnp.sum(jnp.where(chosen, route_weights[:, :, None], 0.0), axis=1)
    if capacity >= streams:
        blocks = [normed] * experts_count
    else:
        named = jnp.any(chosen, axis=1).astype(jnp.int32)
        rank = jnp.cumsum(named, axis=0) - named
        slots = jnp.arange(capacity, dtype=jnp.int32)
        placed = (named == 1)[None, :, :] & (rank[None, :, :] == slots[:, None, None])
        packed = jnp.einsum(
            "ctk,td->kcd",
            placed.astype(jnp.bfloat16),
            normed,
            preferred_element_type=jnp.float32,
        ).astype(jnp.bfloat16)
        blocks = [packed[index] for index in range(experts_count)]
    chips = SPLIT // CORES
    distances = far_first(experts_count)
    if direct:
        planes = {k: swap(blocks[k], k * SPLIT, devices) for k in distances}
        column = [blocks[0]] + [planes[k] for k in range(1, experts_count)]
    else:
        column = outer_exchange(blocks, devices)
    near = {0: jnp.concatenate(column, axis=0)}
    for step in range(1, chips):
        near[step] = swap(near[0], CORES * step, devices)
    other_in = swap(w_in, 1, devices)
    w_out = bring(w_out)
    other_out = swap(w_out, 1, devices)
    parts = feed_forward(
        [near[step] for step in range(chips)], [(w_in, w_out), (other_in, other_out)]
    )
    total = parts[0]
    for step in range(1, chips):
        given = swap(parts[step], CORES * step, devices)
        total = total + given.astype(jnp.float32)
    total = total.reshape(experts_count, capacity, width)
    result = mixed
    sent = total.astype(jnp.bfloat16)
    if direct:
        back = {k: swap(sent[k], k * SPLIT, devices) for k in distances}
        parts = [total[0]] + [back[k].astype(jnp.float32) for k in range(1, experts_count)]
    else:
        back = outer_exchange([sent[k] for k in range(experts_count)], devices)
        parts = [part.astype(jnp.float32) for part in back]
    for k, part in enumerate(parts):
        if capacity < streams:
            part = jnp.einsum(
                "ct,cd->td",
                placed[:, :, k].astype(jnp.float32),
                part,
                precision=lax.Precision.HIGHEST,
                preferred_element_type=jnp.float32,
            )
        result = result + weights[:, k : k + 1] * part
    return result.astype(jnp.bfloat16)


def solution(mesh):
    placed = (
        P(("group", "expert"), None),
        P(("group", "expert"), None),
        P(("group", "expert"), None, None),
        P(("group", "expert"), None, None),
        P(("group", "expert")),
        P(),
        P(None, "expert"),
        P("expert", None),
        P(("group", "expert"), None),
        P(("group", "expert"), None),
    )
    return jax.shard_map(
        step_on_device,
        mesh=mesh,
        in_specs=placed,
        out_specs=P(("group", "expert"), None),
        check_vma=False,
    )
```

```python
import jax
import jax.numpy as jnp
from jax import lax
from jax.experimental import pallas as pl
from jax.experimental.pallas import tpu as pltpu
from jax.sharding import PartitionSpec as P

HEADS = 16
SPLIT = 8
CORES = 2
VMEM_LIMIT = 16 * 1024 * 1024


def swap(value, distance, devices):
    pairs = [(source, source ^ distance) for source in range(devices)]
    return lax.ppermute(value, "expert", pairs)


def outer_exchange(blocks, devices):
    moved = lax.all_to_all(
        jnp.stack(blocks),
        "expert",
        split_axis=0,
        concat_axis=0,
        tiled=True,
        axis_index_groups=[list(range(inner, devices, SPLIT)) for inner in range(SPLIT)],
    )
    return [moved[index] for index in range(len(blocks))]


def far_first(count):
    return list(range(count - 1, 0, -1))


def attend_kernel(lengths_in, hidden_in, query_in, keys, values, gain_in, w_in_from, mixed, normed, w_in, lengths, hidden, query, gain, key_buf, value_buf, score_buf, small_sem, key_sem, value_sem):
    streams, width = hidden.shape
    span = key_buf.shape[1]
    head_size = width // HEADS
    small = [
        pltpu.make_async_copy(query_in, query, small_sem.at[0]),
        pltpu.make_async_copy(lengths_in, lengths, small_sem.at[1]),
        pltpu.make_async_copy(hidden_in, hidden, small_sem.at[2]),
        pltpu.make_async_copy(gain_in, gain, small_sem.at[3]),
    ]
    key_copy = pltpu.make_async_copy(keys, key_buf, key_sem)
    value_copy = pltpu.make_async_copy(values, value_buf, value_sem)
    weight_copy = pltpu.make_async_copy(w_in_from, w_in, small_sem.at[4])
    for copy in small + [key_copy, value_copy, weight_copy]:
        copy.start()
    owner = lax.broadcasted_iota(jnp.int32, (HEADS, width), 1) // head_size
    own = owner == lax.broadcasted_iota(jnp.int32, (HEADS, width), 0)
    position = lax.broadcasted_iota(jnp.int32, (HEADS, span), 1)
    small[0].wait()
    small[1].wait()
    key_copy.wait()
    for b in range(streams):
        spread = jnp.where(own, query[b : b + 1, :].astype(jnp.float32), 0.0).astype(jnp.bfloat16)
        scores = lax.dot_general(spread, key_buf[b], (((1,), (1,)), ((), ())), preferred_element_type=jnp.float32)
        scores = scores / jnp.sqrt(jnp.float32(head_size))
        score_buf[b * HEADS : (b + 1) * HEADS, :] = jnp.where(position < lengths[b], scores, -1e30)
    scores = score_buf[...]
    expo = jnp.exp(scores - jnp.max(scores, axis=-1, keepdims=True))
    score_buf[...] = expo / jnp.sum(expo, axis=-1, keepdims=True)
    value_copy.wait()
    for b in range(streams):
        probabilities = score_buf[b * HEADS : (b + 1) * HEADS, :].astype(jnp.bfloat16)
        every = jnp.dot(probabilities, value_buf[b], preferred_element_type=jnp.float32)
        for h in range(HEADS):
            lanes = slice(h * head_size, (h + 1) * head_size)
            mixed[b : b + 1, lanes] = every[h : h + 1, lanes]
    small[2].wait()
    small[3].wait()
    total = hidden[...].astype(jnp.float32) + mixed[...]
    mixed[...] = total
    centered = total - jnp.mean(total, axis=-1, keepdims=True)
    variance = jnp.mean(centered * centered, axis=-1, keepdims=True)
    normed[...] = (centered * lax.rsqrt(variance + 1e-05) * gain[...]).astype(jnp.bfloat16)
    weight_copy.wait()


def attend(
    hidden_state,
    cross_query,
    source_keys,
    source_values,
    src_lengths,
    norm_gain,
    w_in,
):
    streams, width = hidden_state.shape
    span = source_keys.shape[1]
    arrays = (
        src_lengths,
        hidden_state,
        cross_query,
        source_keys,
        source_values,
        norm_gain.reshape(1, width),
        w_in,
    )
    vmem = pl.BlockSpec(memory_space=pltpu.VMEM)
    hbm = pl.BlockSpec(memory_space=pltpu.HBM)
    return pl.pallas_call(
        attend_kernel,
        out_shape=(
            pltpu.VMEM((streams, width), jnp.float32),
            pltpu.VMEM((streams, width), jnp.bfloat16),
            pltpu.VMEM(w_in.shape, w_in.dtype),
        ),
        in_specs=[hbm] * 7,
        out_specs=(vmem,) * 3,
        scratch_shapes=[
            pltpu.SMEM((streams,), jnp.int32),
            pltpu.VMEM((streams, width), hidden_state.dtype),
            pltpu.VMEM((streams, width), cross_query.dtype),
            pltpu.VMEM((1, width), norm_gain.dtype),
            pltpu.VMEM((streams, span, width), source_keys.dtype),
            pltpu.VMEM((streams, span, width), source_values.dtype),
            pltpu.VMEM((streams * HEADS, span), jnp.float32),
            pltpu.SemaphoreType.DMA((5,)),
            pltpu.SemaphoreType.DMA(()),
            pltpu.SemaphoreType.DMA(()),
        ],
        compiler_params=pltpu.CompilerParams(vmem_limit_bytes=VMEM_LIMIT),
    )(*[pltpu.with_memory_space_constraint(array, pltpu.HBM) for array in arrays])


def bring(array):
    def kernel(source, target, sem):
        copy = pltpu.make_async_copy(source, target, sem)
        copy.start()
        copy.wait()

    return pl.pallas_call(
        kernel,
        out_shape=pltpu.VMEM(array.shape, array.dtype),
        in_specs=[pl.BlockSpec(memory_space=pltpu.HBM)],
        out_specs=pl.BlockSpec(memory_space=pltpu.VMEM),
        scratch_shapes=[pltpu.SemaphoreType.DMA(())],
        compiler_params=pltpu.CompilerParams(vmem_limit_bytes=VMEM_LIMIT),
    )(pltpu.with_memory_space_constraint(array, pltpu.HBM))


def feed_forward(rows, weights):
    kinds = [jnp.float32] + [jnp.bfloat16] * (len(rows) - 1)
    height, width = rows[0].shape

    def kernel(*refs):
        row_refs = refs[: len(rows)]
        weight_refs = refs[len(rows) : len(rows) + 2 * len(weights)]
        out_refs = refs[len(rows) + 2 * len(weights) :]
        stacked = jnp.concatenate([ref[...] for ref in row_refs], axis=0)
        every = None
        for w_in_ref, w_out_ref in zip(weight_refs[::2], weight_refs[1::2]):
            units = jnp.dot(stacked, w_in_ref[...], preferred_element_type=jnp.float32)
            act = jnp.maximum(units, 0.0).astype(jnp.bfloat16)
            some = jnp.dot(act, w_out_ref[...], preferred_element_type=jnp.float32)
            every = some if every is None else every + some
        for block, ref in enumerate(out_refs):
            ref[...] = every[block * height : (block + 1) * height].astype(kinds[block])

    vmem = pl.BlockSpec(memory_space=pltpu.VMEM)
    flat = [array for pair in weights for array in pair]
    size = sum(array.size for array in flat)
    return pl.pallas_call(
        kernel,
        out_shape=[jax.ShapeDtypeStruct((height, width), kind) for kind in kinds],
        in_specs=[vmem] * (len(rows) + len(flat)),
        out_specs=[vmem] * len(rows),
        compiler_params=pltpu.CompilerParams(vmem_limit_bytes=VMEM_LIMIT),
        cost_estimate=pl.CostEstimate(
            flops=2 * len(rows) * height * size, transcendentals=0, bytes_accessed=2 * size
        ),
    )(*rows, *flat)


def step_on_device(
    hidden_state,
    cross_query,
    source_keys,
    source_values,
    src_lengths,
    norm_gain,
    w_in,
    w_out,
    expert_ids,
    route_weights,
):
    streams, width = hidden_state.shape
    devices = lax.axis_size("expert")
    experts_count = devices // SPLIT
    capacity = max(2, min(streams, 4 * streams * SPLIT // devices))
    direct = experts_count <= 4
    group = lax.shift_right_logical(lax.axis_index("expert"), SPLIT.bit_length() - 1)
    group, src_lengths = lax.optimization_barrier((group, src_lengths))
    mixed, normed, w_in = attend(
        hidden_state,
        cross_query,
        source_keys,
        source_values,
        src_lengths,
        norm_gain,
        w_in,
    )
    order = jnp.arange(experts_count, dtype=jnp.int32)
    if direct:
        order = order ^ group
    chosen = expert_ids[:, :, None] == order[None, None, :]
    weights = jnp.sum(jnp.where(chosen, route_weights[:, :, None], 0.0), axis=1)
    if capacity >= streams:
        blocks = [normed] * experts_count
    else:
        named = jnp.any(chosen, axis=1).astype(jnp.int32)
        rank = jnp.cumsum(named, axis=0) - named
        slots = jnp.arange(capacity, dtype=jnp.int32)
        placed = (named == 1)[None, :, :] & (rank[None, :, :] == slots[:, None, None])
        packed = jnp.einsum(
            "ctk,td->kcd",
            placed.astype(jnp.bfloat16),
            normed,
            preferred_element_type=jnp.float32,
        ).astype(jnp.bfloat16)
        blocks = [packed[index] for index in range(experts_count)]
    chips = SPLIT // CORES
    distances = far_first(experts_count)
    if direct:
        planes = {k: swap(blocks[k], k * SPLIT, devices) for k in distances}
        column = [blocks[0]] + [planes[k] for k in range(1, experts_count)]
    else:
        column = outer_exchange(blocks, devices)
    near = {0: jnp.concatenate(column, axis=0)}
    for step in range(1, chips):
        near[step] = swap(near[0], CORES * step, devices)
    other_in = swap(w_in, 1, devices)
    w_out = bring(w_out)
    other_out = swap(w_out, 1, devices)
    parts = feed_forward(
        [near[step] for step in range(chips)], [(w_in, w_out), (other_in, other_out)]
    )
    total = parts[0]
    for step in range(1, chips):
        given = swap(parts[step], CORES * step, devices)
        total = total + given.astype(jnp.float32)
    total = total.reshape(experts_count, capacity, width)
    result = mixed
    sent = total.astype(jnp.bfloat16)
    if direct:
        back = {k: swap(sent[k], k * SPLIT, devices) for k in distances}
        parts = [total[0]] + [back[k].astype(jnp.float32) for k in range(1, experts_count)]
    else:
        back = outer_exchange([sent[k] for k in range(experts_count)], devices)
        parts = [part.astype(jnp.float32) for part in back]
    for k, part in enumerate(parts):
        if capacity < streams:
            part = jnp.einsum(
                "ct,cd->td",
                placed[:, :, k].astype(jnp.float32),
                part,
                precision=lax.Precision.HIGHEST,
                preferred_element_type=jnp.float32,
            )
        result = result + weights[:, k : k + 1] * part
    return result.astype(jnp.bfloat16)


def solution(mesh):
    placed = (
        P(("group", "expert"), None),
        P(("group", "expert"), None),
        P(("group", "expert"), None, None),
        P(("group", "expert"), None, None),
        P(("group", "expert")),
        P(),
        P(None, "expert"),
        P("expert", None),
        P(("group", "expert"), None),
        P(("group", "expert"), None),
    )
    return jax.shard_map(
        step_on_device,
        mesh=mesh,
        in_specs=placed,
        out_specs=P(("group", "expert"), None),
        check_vma=False,
    )
```

```python
import jax
import jax.numpy as jnp
from jax import lax
from jax.experimental import pallas as pl
from jax.experimental.pallas import tpu as pltpu
from jax.sharding import PartitionSpec as P

HEADS = 16
SPLIT = 8
CORES = 2
VMEM_LIMIT = 16 * 1024 * 1024


def swap(value, distance, devices):
    pairs = [(source, source ^ distance) for source in range(devices)]
    return lax.ppermute(value, "expert", pairs)


def chip_swap(value, step, devices):
    orders = [chip_order(core) for core in range(CORES)]
    pairs = [
        (source, source ^ (CORES * orders[source % CORES][step - 1])) for source in range(devices)
    ]
    return lax.ppermute(value, "expert", pairs)


def chip_order(core):
    chips = SPLIT // CORES
    nearer = list(range(1, chips - 1))
    return [chips - 1] + (nearer if core == 0 else nearer[::-1])


def outer_exchange(blocks, devices):
    moved = lax.all_to_all(
        jnp.stack(blocks),
        "expert",
        split_axis=0,
        concat_axis=0,
        tiled=True,
        axis_index_groups=[list(range(inner, devices, SPLIT)) for inner in range(SPLIT)],
    )
    return [moved[index] for index in range(len(blocks))]


def far_first(count):
    return list(range(count - 1, 0, -1))


def attend_kernel(lengths_in, hidden_in, query_in, keys, values, gain_in, w_in_from, mixed, normed, w_in, lengths, hidden, query, gain, key_buf, value_buf, score_buf, small_sem, key_sem, value_sem):
    streams, width = hidden.shape
    span = key_buf.shape[1]
    head_size = width // HEADS
    small = [
        pltpu.make_async_copy(query_in, query, small_sem.at[0]),
        pltpu.make_async_copy(lengths_in, lengths, small_sem.at[1]),
        pltpu.make_async_copy(hidden_in, hidden, small_sem.at[2]),
        pltpu.make_async_copy(gain_in, gain, small_sem.at[3]),
    ]
    key_copy = pltpu.make_async_copy(keys, key_buf, key_sem)
    value_copy = pltpu.make_async_copy(values, value_buf, value_sem)
    weight_copy = pltpu.make_async_copy(w_in_from, w_in, small_sem.at[4])
    for copy in small + [key_copy, value_copy, weight_copy]:
        copy.start()
    owner = lax.broadcasted_iota(jnp.int32, (HEADS, width), 1) // head_size
    own = owner == lax.broadcasted_iota(jnp.int32, (HEADS, width), 0)
    position = lax.broadcasted_iota(jnp.int32, (HEADS, span), 1)
    small[0].wait()
    small[1].wait()
    key_copy.wait()
    for b in range(streams):
        spread = jnp.where(own, query[b : b + 1, :].astype(jnp.float32), 0.0).astype(jnp.bfloat16)
        scores = lax.dot_general(spread, key_buf[b], (((1,), (1,)), ((), ())), preferred_element_type=jnp.float32)
        scores = scores / jnp.sqrt(jnp.float32(head_size))
        score_buf[b * HEADS : (b + 1) * HEADS, :] = jnp.where(position < lengths[b], scores, -1e30)
    scores = score_buf[...]
    expo = jnp.exp(scores - jnp.max(scores, axis=-1, keepdims=True))
    score_buf[...] = expo / jnp.sum(expo, axis=-1, keepdims=True)
    value_copy.wait()
    for b in range(streams):
        probabilities = score_buf[b * HEADS : (b + 1) * HEADS, :].astype(jnp.bfloat16)
        every = jnp.dot(probabilities, value_buf[b], preferred_element_type=jnp.float32)
        for h in range(HEADS):
            lanes = slice(h * head_size, (h + 1) * head_size)
            mixed[b : b + 1, lanes] = every[h : h + 1, lanes]
    small[2].wait()
    small[3].wait()
    total = hidden[...].astype(jnp.float32) + mixed[...]
    mixed[...] = total
    centered = total - jnp.mean(total, axis=-1, keepdims=True)
    variance = jnp.mean(centered * centered, axis=-1, keepdims=True)
    normed[...] = (centered * lax.rsqrt(variance + 1e-05) * gain[...]).astype(jnp.bfloat16)
    weight_copy.wait()


def attend(
    hidden_state,
    cross_query,
    source_keys,
    source_values,
    src_lengths,
    norm_gain,
    w_in,
):
    streams, width = hidden_state.shape
    span = source_keys.shape[1]
    arrays = (
        src_lengths,
        hidden_state,
        cross_query,
        source_keys,
        source_values,
        norm_gain.reshape(1, width),
        w_in,
    )
    vmem = pl.BlockSpec(memory_space=pltpu.VMEM)
    hbm = pl.BlockSpec(memory_space=pltpu.HBM)
    return pl.pallas_call(
        attend_kernel,
        out_shape=(
            pltpu.VMEM((streams, width), jnp.float32),
            pltpu.VMEM((streams, width), jnp.bfloat16),
            pltpu.VMEM(w_in.shape, w_in.dtype),
        ),
        in_specs=[hbm] * 7,
        out_specs=(vmem,) * 3,
        scratch_shapes=[
            pltpu.SMEM((streams,), jnp.int32),
            pltpu.VMEM((streams, width), hidden_state.dtype),
            pltpu.VMEM((streams, width), cross_query.dtype),
            pltpu.VMEM((1, width), norm_gain.dtype),
            pltpu.VMEM((streams, span, width), source_keys.dtype),
            pltpu.VMEM((streams, span, width), source_values.dtype),
            pltpu.VMEM((streams * HEADS, span), jnp.float32),
            pltpu.SemaphoreType.DMA((5,)),
            pltpu.SemaphoreType.DMA(()),
            pltpu.SemaphoreType.DMA(()),
        ],
        compiler_params=pltpu.CompilerParams(vmem_limit_bytes=VMEM_LIMIT),
    )(*[pltpu.with_memory_space_constraint(array, pltpu.HBM) for array in arrays])


def bring(array):
    def kernel(source, target, sem):
        copy = pltpu.make_async_copy(source, target, sem)
        copy.start()
        copy.wait()

    return pl.pallas_call(
        kernel,
        out_shape=pltpu.VMEM(array.shape, array.dtype),
        in_specs=[pl.BlockSpec(memory_space=pltpu.HBM)],
        out_specs=pl.BlockSpec(memory_space=pltpu.VMEM),
        scratch_shapes=[pltpu.SemaphoreType.DMA(())],
        compiler_params=pltpu.CompilerParams(vmem_limit_bytes=VMEM_LIMIT),
    )(pltpu.with_memory_space_constraint(array, pltpu.HBM))


def feed_forward(rows, weights, cuts):
    kinds = [jnp.float32] + [jnp.bfloat16] * (len(rows) - 1)
    height, width = rows[0].shape
    parts = [(block, start, end) for block in range(len(rows)) for start, end in cuts]

    def kernel(*refs):
        row_refs = refs[: len(rows)]
        weight_refs = refs[len(rows) : len(rows) + 2 * len(weights)]
        out_refs = refs[len(rows) + 2 * len(weights) :]
        stacked = jnp.concatenate([ref[...] for ref in row_refs], axis=0)
        every = None
        for w_in_ref, w_out_ref in zip(weight_refs[::2], weight_refs[1::2]):
            units = jnp.dot(stacked, w_in_ref[...], preferred_element_type=jnp.float32)
            act = jnp.maximum(units, 0.0).astype(jnp.bfloat16)
            some = jnp.dot(act, w_out_ref[...], preferred_element_type=jnp.float32)
            every = some if every is None else every + some
        for ref, (block, start, end) in zip(out_refs, parts):
            ref[...] = every[block * height + start : block * height + end].astype(kinds[block])

    vmem = pl.BlockSpec(memory_space=pltpu.VMEM)
    flat = [array for pair in weights for array in pair]
    size = sum(array.size for array in flat)
    out = pl.pallas_call(
        kernel,
        out_shape=[
            jax.ShapeDtypeStruct((end - start, width), kinds[block]) for block, start, end in parts
        ],
        in_specs=[vmem] * (len(rows) + len(flat)),
        out_specs=[vmem] * len(parts),
        compiler_params=pltpu.CompilerParams(vmem_limit_bytes=VMEM_LIMIT),
        cost_estimate=pl.CostEstimate(
            flops=2 * len(rows) * height * size, transcendentals=0, bytes_accessed=2 * size
        ),
    )(*rows, *flat)
    return [out[block * len(cuts) : (block + 1) * len(cuts)] for block in range(len(rows))]


def step_on_device(
    hidden_state,
    cross_query,
    source_keys,
    source_values,
    src_lengths,
    norm_gain,
    w_in,
    w_out,
    expert_ids,
    route_weights,
):
    streams, width = hidden_state.shape
    devices = lax.axis_size("expert")
    experts_count = devices // SPLIT
    capacity = max(2, min(streams, 4 * streams * SPLIT // devices))
    direct = experts_count <= 4
    group = lax.shift_right_logical(lax.axis_index("expert"), SPLIT.bit_length() - 1)
    group, src_lengths = lax.optimization_barrier((group, src_lengths))
    mixed, normed, w_in = attend(
        hidden_state,
        cross_query,
        source_keys,
        source_values,
        src_lengths,
        norm_gain,
        w_in,
    )
    order = jnp.arange(experts_count, dtype=jnp.int32)
    if direct:
        order = order ^ group
    chosen = expert_ids[:, :, None] == order[None, None, :]
    weights = jnp.sum(jnp.where(chosen, route_weights[:, :, None], 0.0), axis=1)
    if capacity >= streams:
        blocks = [normed] * experts_count
    else:
        named = jnp.any(chosen, axis=1).astype(jnp.int32)
        rank = jnp.cumsum(named, axis=0) - named
        slots = jnp.arange(capacity, dtype=jnp.int32)
        placed = (named == 1)[None, :, :] & (rank[None, :, :] == slots[:, None, None])
        packed = jnp.einsum(
            "ctk,td->kcd",
            placed.astype(jnp.bfloat16),
            normed,
            preferred_element_type=jnp.float32,
        ).astype(jnp.bfloat16)
        blocks = [packed[index] for index in range(experts_count)]
    chips = SPLIT // CORES
    distances = far_first(experts_count)
    if direct:
        planes = {k: swap(blocks[k], k * SPLIT, devices) for k in distances}
        column = [blocks[0]] + [planes[k] for k in range(1, experts_count)]
    else:
        column = outer_exchange(blocks, devices)
    near = {0: jnp.concatenate(column, axis=0)}
    for step in range(1, chips):
        near[step] = chip_swap(near[0], step, devices)
    other_in = swap(w_in, 1, devices)
    w_out = bring(w_out)
    other_out = swap(w_out, 1, devices)
    height = near[0].shape[0]
    cuts = [("reduce_chip", 0, height)]
    if direct:
        cuts = [("reduce_chip", capacity, height), ("reduce_own", 0, capacity)]
    parts = feed_forward(
        [near[step] for step in range(chips)],
        [(w_in, w_out), (other_in, other_out)],
        [(start, end) for _, start, end in cuts],
    )
    sums = {}
    for place, (name, _, _) in enumerate(cuts):
        sums[name] = parts[0][place]
        for step in range(1, chips):
            given = chip_swap(parts[step][place], step, devices)
            sums[name] = sums[name] + given.astype(jnp.float32)
    total = sums["reduce_chip"].reshape(-1, capacity, width)
    result = mixed
    sent = total.astype(jnp.bfloat16)
    if direct:
        back = {k: swap(sent[k - 1], k * SPLIT, devices) for k in distances}
        parts = [sums["reduce_own"]]
        parts += [back[k].astype(jnp.float32) for k in range(1, experts_count)]
    else:
        back = outer_exchange([sent[k] for k in range(experts_count)], devices)
        parts = [part.astype(jnp.float32) for part in back]
    for k, part in enumerate(parts):
        if capacity < streams:
            part = jnp.einsum(
                "ct,cd->td",
                placed[:, :, k].astype(jnp.float32),
                part,
                precision=lax.Precision.HIGHEST,
                preferred_element_type=jnp.float32,
            )
        result = result + weights[:, k : k + 1] * part
    return result.astype(jnp.bfloat16)


def solution(mesh):
    placed = (
        P(("group", "expert"), None),
        P(("group", "expert"), None),
        P(("group", "expert"), None, None),
        P(("group", "expert"), None, None),
        P(("group", "expert")),
        P(),
        P(None, "expert"),
        P("expert", None),
        P(("group", "expert"), None),
        P(("group", "expert"), None),
    )
    return jax.shard_map(
        step_on_device,
        mesh=mesh,
        in_specs=placed,
        out_specs=P(("group", "expert"), None),
        check_vma=False,
    )
```

```python
import jax
import jax.numpy as jnp
from jax import lax
from jax.experimental import pallas as pl
from jax.experimental.pallas import tpu as pltpu
from jax.sharding import PartitionSpec as P

HEADS = 16
SPLIT = 8
CORES = 2
VMEM_LIMIT = 16 * 1024 * 1024


def swap(value, distance, devices):
    pairs = [(source, source ^ distance) for source in range(devices)]
    return lax.ppermute(value, "expert", pairs)


def chip_swap(value, step, devices):
    orders = [chip_order(core) for core in range(CORES)]
    pairs = [
        (source, source ^ (CORES * orders[source % CORES][step - 1])) for source in range(devices)
    ]
    return lax.ppermute(value, "expert", pairs)


def chip_order(core):
    chips = SPLIT // CORES
    nearer = list(range(1, chips - 1))
    return [chips - 1] + (nearer if core == 0 else nearer[::-1])


def outer_exchange(blocks, devices):
    moved = lax.all_to_all(
        jnp.stack(blocks),
        "expert",
        split_axis=0,
        concat_axis=0,
        tiled=True,
        axis_index_groups=[list(range(inner, devices, SPLIT)) for inner in range(SPLIT)],
    )
    return [moved[index] for index in range(len(blocks))]


def far_first(count):
    return list(range(count - 1, 0, -1))


def attend_kernel(lengths_in, hidden_in, query_in, keys, values, gain_in, w_in_from, mixed, normed, w_in, lengths, hidden, query, gain, key_buf, value_buf, score_buf, small_sem, key_sem, value_sem):
    streams, width = hidden.shape
    span = key_buf.shape[1]
    head_size = width // HEADS
    small = [
        pltpu.make_async_copy(query_in, query, small_sem.at[0]),
        pltpu.make_async_copy(lengths_in, lengths, small_sem.at[1]),
        pltpu.make_async_copy(hidden_in, hidden, small_sem.at[2]),
        pltpu.make_async_copy(gain_in, gain, small_sem.at[3]),
    ]
    key_copy = pltpu.make_async_copy(keys, key_buf, key_sem)
    value_copy = pltpu.make_async_copy(values, value_buf, value_sem)
    weight_copy = pltpu.make_async_copy(w_in_from, w_in, small_sem.at[4])
    for copy in small + [key_copy, value_copy, weight_copy]:
        copy.start()
    owner = lax.broadcasted_iota(jnp.int32, (HEADS, width), 1) // head_size
    own = owner == lax.broadcasted_iota(jnp.int32, (HEADS, width), 0)
    position = lax.broadcasted_iota(jnp.int32, (HEADS, span), 1)
    small[0].wait()
    small[1].wait()
    key_copy.wait()
    for b in range(streams):
        spread = jnp.where(own, query[b : b + 1, :].astype(jnp.float32), 0.0).astype(jnp.bfloat16)
        scores = lax.dot_general(spread, key_buf[b], (((1,), (1,)), ((), ())), preferred_element_type=jnp.float32)
        scores = scores / jnp.sqrt(jnp.float32(head_size))
        score_buf[b * HEADS : (b + 1) * HEADS, :] = jnp.where(position < lengths[b], scores, -1e30)
    scores = score_buf[...]
    expo = jnp.exp(scores - jnp.max(scores, axis=-1, keepdims=True))
    score_buf[...] = expo / jnp.sum(expo, axis=-1, keepdims=True)
    value_copy.wait()
    for b in range(streams):
        probabilities = score_buf[b * HEADS : (b + 1) * HEADS, :].astype(jnp.bfloat16)
        every = jnp.dot(probabilities, value_buf[b], preferred_element_type=jnp.float32)
        for h in range(HEADS):
            lanes = slice(h * head_size, (h + 1) * head_size)
            mixed[b : b + 1, lanes] = every[h : h + 1, lanes]
    small[2].wait()
    small[3].wait()
    total = hidden[...].astype(jnp.float32) + mixed[...]
    mixed[...] = total
    centered = total - jnp.mean(total, axis=-1, keepdims=True)
    variance = jnp.mean(centered * centered, axis=-1, keepdims=True)
    normed[...] = (centered * lax.rsqrt(variance + 1e-05) * gain[...]).astype(jnp.bfloat16)
    weight_copy.wait()


def attend(
    hidden_state,
    cross_query,
    source_keys,
    source_values,
    src_lengths,
    norm_gain,
    w_in,
):
    streams, width = hidden_state.shape
    span = source_keys.shape[1]
    arrays = (
        src_lengths,
        hidden_state,
        cross_query,
        source_keys,
        source_values,
        norm_gain.reshape(1, width),
        w_in,
    )
    vmem = pl.BlockSpec(memory_space=pltpu.VMEM)
    hbm = pl.BlockSpec(memory_space=pltpu.HBM)
    return pl.pallas_call(
        attend_kernel,
        out_shape=(
            pltpu.VMEM((streams, width), jnp.float32),
            pltpu.VMEM((streams, width), jnp.bfloat16),
            pltpu.VMEM(w_in.shape, w_in.dtype),
        ),
        in_specs=[hbm] * 7,
        out_specs=(vmem,) * 3,
        scratch_shapes=[
            pltpu.SMEM((streams,), jnp.int32),
            pltpu.VMEM((streams, width), hidden_state.dtype),
            pltpu.VMEM((streams, width), cross_query.dtype),
            pltpu.VMEM((1, width), norm_gain.dtype),
            pltpu.VMEM((streams, span, width), source_keys.dtype),
            pltpu.VMEM((streams, span, width), source_values.dtype),
            pltpu.VMEM((streams * HEADS, span), jnp.float32),
            pltpu.SemaphoreType.DMA((5,)),
            pltpu.SemaphoreType.DMA(()),
            pltpu.SemaphoreType.DMA(()),
        ],
        compiler_params=pltpu.CompilerParams(vmem_limit_bytes=VMEM_LIMIT),
    )(*[pltpu.with_memory_space_constraint(array, pltpu.HBM) for array in arrays])


def bring(array):
    def kernel(source, target, sem):
        copy = pltpu.make_async_copy(source, target, sem)
        copy.start()
        copy.wait()

    return pl.pallas_call(
        kernel,
        out_shape=pltpu.VMEM(array.shape, array.dtype),
        in_specs=[pl.BlockSpec(memory_space=pltpu.HBM)],
        out_specs=pl.BlockSpec(memory_space=pltpu.VMEM),
        scratch_shapes=[pltpu.SemaphoreType.DMA(())],
        compiler_params=pltpu.CompilerParams(vmem_limit_bytes=VMEM_LIMIT),
    )(pltpu.with_memory_space_constraint(array, pltpu.HBM))


def feed_forward(rows, weights, cuts):
    kinds = [jnp.float32] + [jnp.bfloat16] * (len(rows) - 1)
    height, width = rows[0].shape
    parts = [(block, start, end) for block in range(len(rows)) for start, end in cuts]

    def kernel(*refs):
        row_refs = refs[: len(rows)]
        weight_refs = refs[len(rows) : len(rows) + 2 * len(weights)]
        out_refs = refs[len(rows) + 2 * len(weights) :]
        stacked = jnp.concatenate([ref[...] for ref in row_refs], axis=0)
        every = None
        for w_in_ref, w_out_ref in zip(weight_refs[::2], weight_refs[1::2]):
            units = jnp.dot(stacked, w_in_ref[...], preferred_element_type=jnp.float32)
            act = jnp.maximum(units, 0.0).astype(jnp.bfloat16)
            some = jnp.dot(act, w_out_ref[...], preferred_element_type=jnp.float32)
            every = some if every is None else every + some
        for ref, (block, start, end) in zip(out_refs, parts):
            ref[...] = every[block * height + start : block * height + end].astype(kinds[block])

    vmem = pl.BlockSpec(memory_space=pltpu.VMEM)
    flat = [array for pair in weights for array in pair]
    size = sum(array.size for array in flat)
    out = pl.pallas_call(
        kernel,
        out_shape=[
            jax.ShapeDtypeStruct((end - start, width), kinds[block]) for block, start, end in parts
        ],
        in_specs=[vmem] * (len(rows) + len(flat)),
        out_specs=[vmem] * len(parts),
        compiler_params=pltpu.CompilerParams(vmem_limit_bytes=VMEM_LIMIT),
        cost_estimate=pl.CostEstimate(
            flops=2 * len(rows) * height * size, transcendentals=0, bytes_accessed=2 * size
        ),
    )(*rows, *flat)
    return [out[block * len(cuts) : (block + 1) * len(cuts)] for block in range(len(rows))]


def step_on_device(
    hidden_state,
    cross_query,
    source_keys,
    source_values,
    src_lengths,
    norm_gain,
    w_in,
    w_out,
    expert_ids,
    route_weights,
):
    streams, width = hidden_state.shape
    devices = lax.axis_size("expert")
    experts_count = devices // SPLIT
    capacity = max(2, min(streams, 4 * streams * SPLIT // devices))
    direct = experts_count <= 4
    group = lax.shift_right_logical(lax.axis_index("expert"), SPLIT.bit_length() - 1)
    group, src_lengths = lax.optimization_barrier((group, src_lengths))
    mixed, normed, w_in = attend(
        hidden_state,
        cross_query,
        source_keys,
        source_values,
        src_lengths,
        norm_gain,
        w_in,
    )
    order = jnp.arange(experts_count, dtype=jnp.int32)
    if direct:
        order = order ^ group
    chosen = expert_ids[:, :, None] == order[None, None, :]
    weights = jnp.sum(jnp.where(chosen, route_weights[:, :, None], 0.0), axis=1)
    if capacity >= streams:
        blocks = [normed] * experts_count
    else:
        named = jnp.any(chosen, axis=1).astype(jnp.int32)
        rank = jnp.cumsum(named, axis=0) - named
        slots = jnp.arange(capacity, dtype=jnp.int32)
        placed = (named == 1)[None, :, :] & (rank[None, :, :] == slots[:, None, None])
        packed = jnp.einsum(
            "ctk,td->kcd",
            placed.astype(jnp.bfloat16),
            normed,
            preferred_element_type=jnp.float32,
        ).astype(jnp.bfloat16)
        blocks = [packed[index] for index in range(experts_count)]
    chips = SPLIT // CORES
    distances = far_first(experts_count)
    if direct:
        planes = {k: swap(blocks[k], k * SPLIT, devices) for k in distances}
        column = [blocks[0]] + [planes[k] for k in range(1, experts_count)]
    else:
        column = outer_exchange(blocks, devices)
    near = {0: jnp.concatenate(column, axis=0)}
    for step in range(1, chips):
        near[step] = chip_swap(near[0], step, devices)
    other_in = swap(w_in, 1, devices)
    w_out = bring(w_out)
    other_out = swap(w_out, 1, devices)
    height = near[0].shape[0]
    nearer = experts_count // 2
    cuts = [("reduce_chip", 0, height)]
    if direct:
        split = nearer * capacity
        cuts = [("reduce_chip", split, height), ("reduce_own", 0, split)]
    parts = feed_forward(
        [near[step] for step in range(chips)],
        [(w_in, w_out), (other_in, other_out)],
        [(start, end) for _, start, end in cuts],
    )
    sums = {}
    for place, (name, _, _) in enumerate(cuts):
        sums[name] = parts[0][place]
        for step in range(1, chips):
            given = chip_swap(parts[step][place], step, devices)
            sums[name] = sums[name] + given.astype(jnp.float32)
    total = [sums[name].reshape(-1, capacity, width) for name, _, _ in cuts[::-1]]
    total = [rows[k] for rows in total for k in range(rows.shape[0])]
    sent = [rows.astype(jnp.bfloat16) for rows in total]
    result = mixed
    if direct:
        back = {k: swap(sent[k], k * SPLIT, devices) for k in distances}
        parts = [total[0]] + [back[k].astype(jnp.float32) for k in range(1, experts_count)]
    else:
        back = outer_exchange(sent, devices)
        parts = [part.astype(jnp.float32) for part in back]
    for k, part in enumerate(parts):
        if capacity < streams:
            part = jnp.einsum(
                "ct,cd->td",
                placed[:, :, k].astype(jnp.float32),
                part,
                precision=lax.Precision.HIGHEST,
                preferred_element_type=jnp.float32,
            )
        result = result + weights[:, k : k + 1] * part
    return result.astype(jnp.bfloat16)


def solution(mesh):
    placed = (
        P(("group", "expert"), None),
        P(("group", "expert"), None),
        P(("group", "expert"), None, None),
        P(("group", "expert"), None, None),
        P(("group", "expert")),
        P(),
        P(None, "expert"),
        P("expert", None),
        P(("group", "expert"), None),
        P(("group", "expert"), None),
    )
    return jax.shard_map(
        step_on_device,
        mesh=mesh,
        in_specs=placed,
        out_specs=P(("group", "expert"), None),
        check_vma=False,
    )
```
